256 devices in a mesh: dp: 8 (over y, x_hi), proto: 16 (over z, core), crop: 2 (over x_lo).
Axes of the slice: x: 4 (x_hi: 2, x_lo: 2; x = x_hi * 2 + x_lo), y: 4, z: 8, core: 2. Of those that a mesh axis runs over, the one named last changes fastest.
Arguments:
- embeddings: bfloat16 [2048, 2, 4, 256], P(('dp', 'proto'), 'crop'), may hold values from -2 to 2
- codes: bfloat16 [2048, 2, 65536], P('dp', 'crop', 'proto'), may hold values from 0 to 1, as said below
- prototypes: bfloat16 [16, 4096, 256], P('proto', ('dp', 'crop')), may hold values from -2 to 2
Outputs:
- grad_emb: float32 [2048, 2, 4, 256], P(('dp', 'proto'), 'crop')
- grad_proto: float32 [16, 4096, 256], P('proto', ('dp', 'crop'))
The draws below stay inside these ranges and needn't reach their ends.
Inputs may be any that keep to these rules, and one draw needn't show every extreme that they name: `codes`: each image's code is a distribution over the prototypes: nonnegative entries that sum to about one over all 65536.
All inputs are finite; a program needn't handle non-finite values.
Results may differ from the reference program's by a relative error of at most 0.0031.
Values may be sent and summed in bfloat16 or wider, within the bound.
No kernel may reach another device: no remote copies, remote signals or barrier semaphores. Data moves between devices by JAX's collectives and lax.ppermute only.
A program may use at most 64 MiB of HBM per device.

```python
import jax
import jax.numpy as jnp
from jax import lax

D = 256
K = 65536
GROUP = 4
BLOCKS = 16
KP = 4096
IMAGES = 2048
N_DP = 8


def shared_direction(key):
    vector = jax.random.normal(jax.random.fold_in(key, 101), (D,), jnp.float32)
    return vector / jnp.sqrt(jnp.sum(vector * vector))


def draw_embeddings(key, part):
    direction = shared_direction(key)
    noise = jax.random.normal(jax.random.fold_in(key, 1), (IMAGES, 2, GROUP, D), jnp.float32) / jnp.sqrt(float(D))
    along = jax.random.uniform(jax.random.fold_in(key, 2), (IMAGES, 2, GROUP, 1), jnp.float32, 0.5, 1.5)
    scale = 0.3
    return jnp.clip(scale * (noise + along * direction), -2.0, 2.0).astype(jnp.bfloat16)


def draw_prototypes(key, part):
    direction = shared_direction(key)
    noise = jax.random.normal(jax.random.fold_in(key, 11), (BLOCKS, KP, D), jnp.float32) / jnp.sqrt(float(D))
    position = jnp.arange(BLOCKS * KP, dtype=jnp.float32).reshape(BLOCKS, KP, 1) / float(K)
    along = 0.35 * position
    scale = 0.25
    return jnp.clip(scale * (noise + along * direction), -2.0, 2.0).astype(jnp.bfloat16)


def draw_codes(key, part):
    logits = 2.5 * jax.random.normal(jax.random.fold_in(key, 22), (IMAGES, 2, K), jnp.float32)
    owner_rows = KP // (N_DP * 2)
    strip = jnp.arange(K, dtype=jnp.int32) % KP // owner_rows // 2
    image_block = jnp.arange(IMAGES, dtype=jnp.int32) // (IMAGES // N_DP)
    paired = (image_block + N_DP // 2) % N_DP
    bump = jnp.where(strip[None, :] == paired[:, None], 4.0, 0.0).astype(jnp.float32)
    return jax.nn.softmax(logits + bump[:, None, :], axis=-1).astype(jnp.bfloat16)


def setup_inputs(seed: int = 0) -> dict:
    key_of = jax.random.split(jax.random.key(seed), 4)
    embeddings = draw_embeddings(jax.random.fold_in(key_of[3], 71), 0)
    codes = draw_codes(jax.random.fold_in(key_of[3], 71), 0)
    prototypes = draw_prototypes(jax.random.fold_in(key_of[3], 71), 0)
    return dict(embeddings=embeddings, codes=codes, prototypes=prototypes)


sharpness_divisor = 0.1
epsilon = 1e-06

def reference(embeddings, codes, prototypes):
    floats = embeddings.astype(jnp.float32)
    emb_norm = jnp.sqrt(lax.optimization_barrier(jnp.sum(floats * floats, axis=-1, keepdims=True)) + epsilon)
    unit_emb = floats / emb_norm
    rounded = unit_emb.astype(jnp.bfloat16)
    proto_float = prototypes.astype(jnp.float32).reshape(K, D)
    proto_norm = jnp.sqrt(lax.optimization_barrier(jnp.sum(proto_float * proto_float, axis=-1, keepdims=True)) + epsilon)
    unit_proto = proto_float / proto_norm
    rescaled_input = unit_proto.astype(jnp.bfloat16)
    as_floats = rounded.astype(jnp.float32)
    local_sum = lax.optimization_barrier(jnp.sum(as_floats[:, :, 1:, :], axis=2))
    all_locals = local_sum[:, 0] + local_sum[:, 1]
    target_sums = jnp.stack([as_floats[:, 1, 0] + all_locals, as_floats[:, 0, 0] + all_locals], axis=1).astype(jnp.bfloat16)
    view_results = jnp.where(jnp.arange(GROUP) == 0, 1.0, 2.0).astype(jnp.float32)
    is_global = (jnp.arange(GROUP) == 0)[None, :, None]
    group_images = IMAGES // N_DP

    def one_group(running, dp_index):
        first_image = (dp_index * group_images).astype(jnp.int32)
        code_block = lax.dynamic_slice_in_dim(codes, first_image, group_images, 0)
        emb_block = lax.dynamic_slice_in_dim(rounded, first_image, group_images, 0)
        sum_block = lax.dynamic_slice_in_dim(target_sums, first_image, group_images, 0)
        code_terms = [jnp.dot(code_block[:, code_index], rescaled_input, preferred_element_type=jnp.float32) for code_index in (0, 1)]
        view_gradient_list = []
        for crop_group in range(2):
            view_row_list = emb_block[:, crop_group].reshape(group_images * GROUP, D)
            prototype_scores = jnp.dot(view_row_list, rescaled_input.T, preferred_element_type=jnp.float32) / sharpness_divisor
            exponent = jnp.exp(prototype_scores)
            probs = (exponent / lax.optimization_barrier(jnp.sum(exponent, axis=1, keepdims=True))).astype(jnp.bfloat16)
            softened_rows = jnp.dot(probs, rescaled_input, preferred_element_type=jnp.float32).reshape(group_images, GROUP, D)
            weighted = (view_row_list.astype(jnp.float32) * jnp.tile(view_results, group_images)[:, None]).astype(jnp.bfloat16)
            proto_term = jnp.dot(probs.T, weighted, preferred_element_type=jnp.float32)
            proto_term = proto_term - jnp.dot(code_block[:, crop_group].T, sum_block[:, crop_group], preferred_element_type=jnp.float32)
            running = running + proto_term
            partner = code_terms[1 - crop_group]
            both_terms = code_terms[0] + code_terms[1]
            goal_codes = jnp.where(is_global, partner[:, None, :], both_terms[:, None, :])
            view_gradient_list.append((softened_rows * view_results[None, :, None] - goal_codes) / sharpness_divisor)
        return (running, jnp.stack(view_gradient_list, axis=1))
    running, stacked = lax.scan(one_group, jnp.zeros((K, D), jnp.float32), jnp.arange(N_DP, dtype=jnp.int32))
    score_grad = stacked.reshape(IMAGES, 2, GROUP, D)
    grad_emb = (score_grad - unit_emb * lax.optimization_barrier(jnp.sum(unit_emb * score_grad, axis=-1, keepdims=True))) / emb_norm
    grad_proto = (running - unit_proto * lax.optimization_barrier(jnp.sum(unit_proto * running, axis=-1, keepdims=True))) / proto_norm
    return (grad_emb, grad_proto.reshape(BLOCKS, KP, D))
```

```python
import jax
import jax.numpy as jnp
from jax import lax
from jax.sharding import PartitionSpec as P

sharpness = 10.0
epsilon = 1e-06
grad_scale = 8.0
f16, bf16, f32 = jnp.float16, jnp.bfloat16, jnp.float32


def swapped(value):
    return lax.ppermute(value, "crop", [(0, 1), (1, 0)])


def normalize_rows(values):
    floats = values.astype(f32)
    lengths = jnp.sqrt(jnp.sum(floats * floats, axis=-1, keepdims=True) + epsilon)
    return floats / lengths, lengths


def dot(left, right, dims):
    return lax.dot_general(left, right, ((dims[0], dims[1]), ((), ())), preferred_element_type=f32)


def on_device(embeddings, codes, prototypes):
    n_group = lax.axis_size(("dp", "crop"))
    n_proto = lax.axis_size("proto")
    crops = embeddings.shape[2]
    features = embeddings.shape[3]
    own_images = embeddings.shape[0]
    images = own_images * n_proto
    rows = images * crops
    own_rows = own_images * crops

    raw_proto = lax.all_to_all(
        jnp.broadcast_to(prototypes, (n_group, *prototypes.shape[1:])), ("dp", "crop"), 0, 0
    ).reshape(-1, features)
    raw_emb = lax.all_gather(embeddings.reshape(own_rows, features), "proto", axis=0, tiled=True)

    z = normalize_rows(raw_emb)[0].astype(bf16)
    c = normalize_rows(raw_proto)[0].astype(bf16)
    z_floats = z.astype(f32).reshape(images, crops, features)
    local_sum = jnp.sum(z_floats[:, 1:], axis=1)
    incoming = swapped(z_floats[:, 0] + local_sum)
    target_sum = (local_sum + incoming).astype(bf16)
    code = codes[:, 0]

    exponent = jnp.exp(dot(z, c, ((1,), (1,))) * sharpness)
    local_total = jnp.sum(exponent, axis=1, keepdims=True)
    exponent = exponent.astype(bf16)
    softened = dot(exponent, c, ((1,), (0,))) / local_total
    own_term = dot(code, c, ((1,), (0,)))
    log_total = jnp.log(local_total)
    log_high = log_total.astype(f16)
    log_low = (log_total - log_high.astype(f32)).astype(f16)
    log_pair = jnp.stack([log_high, log_low]).reshape(1, -1, features)
    payload = jnp.concatenate(
        [
            softened.astype(f16).reshape(n_proto, own_rows, features),
            own_term.astype(f16).reshape(n_proto, own_images, features),
            jnp.broadcast_to(log_pair, (n_proto, *log_pair.shape[1:])),
        ],
        axis=1,
    )
    received = lax.all_to_all(payload, "proto", 0, 0).astype(f32)
    logs = received[:, own_rows + own_images :].reshape(n_proto, 2, rows)
    totals_by_block = jnp.exp(logs[:, 0] + logs[:, 1])
    totals = jnp.sum(totals_by_block, axis=0)

    view_results = jnp.where(jnp.arange(crops) == 0, 1.0, 2.0).astype(f32)
    row_weight = jnp.tile(view_results, images)
    weighted = (z.astype(f32) * (row_weight / totals)[:, None]).astype(bf16)
    proto_sum = dot(exponent, weighted, ((0,), (0,))) - dot(code, target_sum, ((0,), (0,)))
    proto_parts = (proto_sum * grad_scale).astype(f16).reshape(n_group, -1, features)
    proto_parts = lax.all_to_all(proto_parts, ("dp", "crop"), 0, 0)

    first = lax.axis_index("proto") * own_rows
    own_share = lax.dynamic_slice_in_dim(
        totals_by_block * (row_weight / totals)[None, :], first, own_rows, 1
    )
    soft_rows = jnp.sum(received[:, :own_rows] * own_share[:, :, None], axis=0)
    soft_rows = soft_rows.reshape(own_images, crops, features)
    own_code_term = jnp.sum(received[:, own_rows : own_rows + own_images], axis=0)
    other_code_term = swapped(own_code_term)
    is_global = (jnp.arange(crops) == 0)[None, :, None]
    assigned = jnp.where(
        is_global, other_code_term[:, None], (own_code_term + other_code_term)[:, None]
    )
    unit_emb, emb_norm = normalize_rows(embeddings[:, 0])
    score_grad = (soft_rows - assigned) * sharpness
    grad_emb = (
        score_grad - unit_emb * jnp.sum(unit_emb * score_grad, axis=-1, keepdims=True)
    ) / emb_norm

    proto_grad = jnp.sum(proto_parts.astype(f32), axis=0) / grad_scale
    unit_proto, proto_norm = normalize_rows(prototypes[0])
    grad_proto = (
        proto_grad - unit_proto * jnp.sum(unit_proto * proto_grad, axis=-1, keepdims=True)
    ) / proto_norm
    return (grad_emb[:, None], grad_proto[None])


def solution(mesh):
    return jax.shard_map(
        on_device,
        mesh=mesh,
        in_specs=(
            P(("dp", "proto"), "crop", None, None),
            P("dp", "crop", "proto"),
            P("proto", ("dp", "crop"), None),
        ),
        out_specs=(P(("dp", "proto"), "crop", None, None), P("proto", ("dp", "crop"), None)),
        check_vma=False,
    )
```

```python
import functools

import jax
import jax.numpy as jnp
from jax import lax
from jax.experimental import pallas as pl
from jax.experimental.pallas import tpu as pltpu
from jax.sharding import PartitionSpec as P


sharpness = 10.0
epsilon = 1e-06
grad_scale = 8.0
unit = 128
side = 4
f16, bf16, f32 = jnp.float16, jnp.bfloat16, jnp.float32
owners = ("dp", "crop")


def swapped(value):
    return lax.ppermute(value, "crop", [(0, 1), (1, 0)])


def ring(value, along, distance):
    pairs = []
    for source in range(side * side):
        y, x = divmod(source, side)
        if along == "y":
            y = (y + distance) % side
        else:
            x = (x + distance) % side
        pairs.append((source, y * side + x))
    return lax.ppermute(value, owners, pairs)


def normalize_rows(values):
    floats = values.astype(f32)
    lengths = jnp.sqrt(jnp.sum(floats * floats, axis=-1, keepdims=True) + epsilon)
    return floats / lengths, lengths


def dot(left, right, left_dim, right_dim):
    return lax.dot_general(
        left, right, (((left_dim,), (right_dim,)), ((), ())), preferred_element_type=f32
    )


def row_weights(totals_ref, crops, own_images):
    totals = jnp.sum(totals_ref[...], axis=0)
    flat = jnp.concatenate([totals[r : r + 1] for r in range(totals.shape[0])], axis=1)
    lane = lax.broadcasted_iota(jnp.int32, flat.shape, 1)
    views = jnp.where((lane // own_images) % crops == 0, 1.0, 2.0).astype(f32)
    return views / flat


def code_columns(code_ref, columns_ref, group):
    parts = []
    for j in range(side):
        first = pl.multiple_of(columns_ref[group * side + j] * unit, unit)
        parts.append(code_ref[:, pl.ds(first, unit)])
    return jnp.concatenate(parts, axis=1)


def embeddings_kernel(raw_ref, z_t_ref, local_ref, outgoing_ref):
    z = normalize_rows(raw_ref[...])[0].astype(bf16).astype(f32)
    features = z.shape[-1]
    local = z[:, 1]
    for crop in range(2, z.shape[1]):
        local = local + z[:, crop]
    local_ref[...] = local.reshape(-1, features)
    outgoing_ref[...] = (z[:, 0] + local).reshape(-1, features)
    z_t_ref[...] = z.reshape(-1, features).T.astype(bf16)


def scores_kernel(*refs, groups, first, last):
    columns_ref, z_t_ref, code_ref = refs[:3]
    refs = refs[3:]
    before = () if first else refs[:3]
    refs = refs[len(before) :]
    raw_refs, refs = refs[: len(groups)], refs[len(groups) :]
    exp_refs, (soft_ref, own_ref, total_ref) = refs[: len(groups)], refs[len(groups) :]

    soft, own, acc = (None, None, None) if first else (ref[...] for ref in before)
    add = lambda a, b: b if a is None else a + b
    for group, raw_ref, exp_ref in zip(groups, raw_refs, exp_refs):
        c = normalize_rows(raw_ref[...])[0].astype(bf16)
        exponent = jnp.exp(dot(c, z_t_ref[...], 1, 0) * sharpness)
        rows = exponent.shape[1]
        acc = add(acc, jnp.sum(exponent.reshape(-1, 8, rows), axis=0))
        exponent = exponent.astype(bf16)
        exp_ref[...] = exponent
        soft = add(soft, dot(c, exponent, 0, 0))
        own = add(own, dot(code_columns(code_ref, columns_ref, group), c, 1, 0))
    soft_ref[...] = soft
    own_ref[...] = own
    if last:
        totals = jnp.sum(acc, axis=0, keepdims=True)
        for r in range(total_ref.shape[0]):
            total_ref[r : r + 1] = totals[:, r * 128 : (r + 1) * 128]
    else:
        total_ref[...] = acc


def prototypes_kernel(*refs, groups, crops, own_images):
    columns_ref, totals_ref, z_t_ref, local_ref, incoming_ref, code_ref = refs[:6]
    exp_refs, out_refs = refs[6 : 6 + len(groups)], refs[6 + len(groups) :]
    weights = row_weights(totals_ref, crops, own_images)
    zw = (z_t_ref[...].astype(f32) * weights).astype(bf16)
    target = (local_ref[...] + incoming_ref[...]).astype(bf16)
    for group, exp_ref, out_ref in zip(groups, exp_refs, out_refs):
        code = code_columns(code_ref, columns_ref, group)
        out_ref[...] = (dot(exp_ref[...], zw, 1, 1) - dot(code, target, 0, 0)) * grad_scale


def rows_kernel(totals_ref, soft_ref, own_ref, out_ref, *, crops, own_images):
    weights = row_weights(totals_ref, crops, own_images)
    own_rows = crops * own_images
    n_proto = out_ref.shape[0]
    features = out_ref.shape[2]
    soft = (soft_ref[...] * weights).T
    out_ref[:, :own_rows] = soft.reshape(n_proto, own_rows, features)
    out_ref[:, own_rows:] = own_ref[...].reshape(n_proto, own_images, features)


def finish_kernel(total_ref, raw_ref, out_ref):
    unit_proto, length = normalize_rows(raw_ref[...])
    grad = total_ref[...] * (1.0 / grad_scale)
    along = jnp.sum(unit_proto * grad, axis=-1, keepdims=True)
    out_ref[...] = (grad - unit_proto * along) / length


def shape(*dims, dtype=f32):
    return jax.ShapeDtypeStruct(dims, dtype)


def call(kernel, out_shape, operands, mib=20, scalars=False):
    kept = pl.BlockSpec(memory_space=pltpu.VMEM)
    specs = [kept] * len(operands)
    if scalars:
        specs[0] = pl.BlockSpec(memory_space=pltpu.SMEM)
    return pl.pallas_call(
        kernel,
        out_shape=out_shape,
        in_specs=specs,
        out_specs=jax.tree.map(lambda _: kept, out_shape),
        compiler_params=pltpu.CompilerParams(vmem_limit_bytes=mib << 20),
    )(*operands)


def on_device(embeddings, codes, prototypes):
    n_proto = lax.axis_size("proto")
    own_images, _, crops, features = embeddings.shape
    images = own_images * n_proto
    rows = images * crops
    own_rows = own_images * crops
    code = codes[:, 0]
    half = prototypes.shape[1] // 2

    place = lax.axis_index(owners)
    y, x = place // side, place % side
    near, far = jnp.arange(side), jnp.arange(side)[:, None]
    columns_a = (((y - near) % side) * side + (x - far) % side) * 2
    columns_b = (((y - far) % side) * side + (x - near) % side) * 2 + 1
    columns = jnp.stack([columns_a, columns_b]).reshape(-1).astype(jnp.int32)
    group_of = lambda kind, d: kind * side + d

    gathered = {}
    first_stage = [[prototypes[0, :half]], [prototypes[0, half:]]]
    for d in (2, 1, 3):
        for kind, along in ((0, "y"), (1, "x")):
            with jax.named_scope("gather_near"):
                first_stage[kind].append(ring(first_stage[kind][0], along, d))

    by_crop = jnp.swapaxes(embeddings[:, 0], 0, 1)
    own_emb = by_crop.reshape(1, own_rows, features)
    with jax.named_scope("gather_rows"):
        raw_emb = lax.all_to_all(
            jnp.broadcast_to(own_emb, (n_proto, own_rows, features)), "proto", 0, 0
        )

    for kind in (0, 1):
        own, opposite, plus, minus = first_stage[kind]
        gathered[kind, 0] = jnp.concatenate([own, plus, opposite, minus])
    for d in (2, 1, 3):
        for kind, along in ((0, "x"), (1, "y")):
            with jax.named_scope("gather_far"):
                gathered[kind, d] = ring(gathered[kind, 0], along, d)

    z_t, local_sum, outgoing = call(
        embeddings_kernel,
        (shape(features, rows, dtype=bf16), shape(images, features), shape(images, features)),
        (raw_emb.reshape(n_proto, crops, own_images, features),),
    )

    exponents = {}
    state = ()
    calls = ((0,), (1, 3), (2,))
    for index, distances in enumerate(calls):
        keys = [(kind, d) for d in distances for kind in (0, 1)]
        last = index == len(calls) - 1
        out_shape = [shape(side * unit, rows, dtype=bf16) for _ in keys]
        out_shape += [shape(features, rows), shape(images, features)]
        out_shape += [shape(rows // 128, 128) if last else shape(8, rows)]
        outs = call(
            functools.partial(
                scores_kernel, groups=[group_of(*k) for k in keys], first=not state, last=last
            ),
            out_shape,
            (columns, z_t, code, *state, *(gathered[k] for k in keys)),
            scalars=True,
            mib=28,
        )
        exponents.update(zip(keys, outs))
        state = tuple(outs[len(keys) :])
        if index == 1:
            outgoing, *state = lax.optimization_barrier((outgoing, *state))
            with jax.named_scope("target_swap"):
                incoming = swapped(outgoing)
    soft, own_term, totals = state
    totals = lax.all_gather(totals, "proto", axis=0, tiled=False)

    kept_parts = {}
    arrived = [[], []]
    for distances in ((2,), (1, 3), (0,)):
        keys = [(kind, d) for d in distances for kind in (0, 1)]
        outs = call(
            functools.partial(
                prototypes_kernel,
                groups=[group_of(*k) for k in keys],
                crops=crops,
                own_images=own_images,
            ),
            [shape(side * unit, features) for _ in keys],
            (columns, totals, z_t, local_sum, incoming, code, *(exponents[k] for k in keys)),
            scalars=True,
            mib=28,
        )
        for (kind, d), out in zip(keys, outs):
            if d == 0:
                kept_parts[kind] = out
            else:
                with jax.named_scope("scatter_far"):
                    arrived[kind].append(ring(out.astype(f16), "xy"[kind], -d))

    soft, own_term, kept_parts = lax.optimization_barrier((soft, own_term, kept_parts))
    row_parts = call(
        functools.partial(rows_kernel, crops=crops, own_images=own_images),
        shape(n_proto, own_rows + own_images, features),
        (totals, soft, own_term),
    )
    with jax.named_scope("row_scatter"):
        row_parts = lax.all_to_all(row_parts.astype(f16), "proto", 0, 0)

    proto_sums = []
    for kind in (0, 1):
        partial_sum = kept_parts[kind]
        for part in arrived[kind]:
            partial_sum = partial_sum + part.astype(f32)
        partial_sum = partial_sum.reshape(side, unit, features)
        total = partial_sum[0]
        for j in (2, 1, 3):
            with jax.named_scope("scatter_near"):
                part = ring(partial_sum[j].astype(f16), "yx"[kind], -j)
            total = total + part.astype(f32)
        proto_sums.append(total)

    row_sums = jnp.sum(row_parts.astype(f32), axis=0)
    own_code_term = row_sums[own_rows:]
    other_code_term = swapped(own_code_term)
    both = own_code_term + other_code_term
    assigned = jnp.stack([other_code_term] + [both] * (crops - 1))
    unit_emb, emb_norm = normalize_rows(by_crop)
    score_grad = (row_sums[:own_rows].reshape(crops, own_images, features) - assigned) * sharpness
    grad_emb = (
        score_grad - unit_emb * jnp.sum(unit_emb * score_grad, axis=-1, keepdims=True)
    ) / emb_norm
    grad_emb = jnp.swapaxes(grad_emb, 0, 1)[:, None]

    grad_proto = call(
        finish_kernel,
        shape(*prototypes.shape[1:]),
        (jnp.concatenate(proto_sums), prototypes[0]),
    )
    return (grad_emb, grad_proto[None])


def solution(mesh):
    return jax.shard_map(
        on_device,
        mesh=mesh,
        in_specs=(
            P(("dp", "proto"), "crop", None, None),
            P("dp", "crop", "proto"),
            P("proto", ("dp", "crop"), None),
        ),
        out_specs=(P(("dp", "proto"), "crop", None, None), P("proto", ("dp", "crop"), None)),
        check_vma=False,
    )
```

```python
import functools

import jax
import jax.numpy as jnp
from jax import lax
from jax.experimental import pallas as pl
from jax.experimental.pallas import tpu as pltpu
from jax.sharding import PartitionSpec as P


sharpness = 10.0
epsilon = 1e-06
grad_scale = 8.0
tile = 512
side = 4
arrivals = (2, 1, 3)
f16, bf16, f32 = jnp.float16, jnp.bfloat16, jnp.float32
owners = ("dp", "crop")


def swapped(value):
    return lax.ppermute(value, "crop", [(0, 1), (1, 0)])


def exchange(value, along, mask):
    step = mask * (side if along == "y" else 1)
    return lax.ppermute(value, owners, [(owner, owner ^ step) for owner in range(side * side)])


def normalize_rows(values):
    floats = values.astype(f32)
    lengths = jnp.sqrt(jnp.sum(floats * floats, axis=-1, keepdims=True) + epsilon)
    return floats / lengths, lengths


def dot(left, right, left_dim, right_dim):
    return lax.dot_general(
        left, right, (((left_dim,), (right_dim,)), ((), ())), preferred_element_type=f32
    )


def row_weights(totals_ref, crops, own_images):
    totals = jnp.sum(totals_ref[...], axis=0)
    flat = jnp.concatenate([totals[r : r + 1] for r in range(totals.shape[0])], axis=1)
    lane = lax.broadcasted_iota(jnp.int32, flat.shape, 1)
    views = jnp.where((lane // own_images) % crops == 0, 1.0, 2.0).astype(f32)
    return views / flat


def code_columns(code_ref, columns_ref, group, index, unit):
    per_tile = tile // unit
    parts = []
    for j in range(per_tile):
        owner = columns_ref[group * side + index * per_tile + j]
        parts.append(code_ref[:, pl.ds(pl.multiple_of(owner * unit, unit), unit)])
    return jnp.concatenate(parts, axis=1)


def embeddings_kernel(raw_ref, z_t_ref, local_ref, outgoing_ref):
    z = normalize_rows(raw_ref[...])[0].astype(bf16).astype(f32)
    features = z.shape[-1]
    local = z[:, 1]
    for crop in range(2, z.shape[1]):
        local = local + z[:, crop]
    local_ref[...] = local.reshape(-1, features)
    outgoing_ref[...] = (z[:, 0] + local).reshape(-1, features)
    z_t_ref[...] = z.reshape(-1, features).T.astype(bf16)


def scores_kernel(*refs, group, unit, first, last):
    columns_ref, z_t_ref, code_ref = refs[:3]
    before = () if first else refs[3:6]
    raw_ref, exp_ref, soft_ref, own_ref, total_ref, acc_ref = refs[3 + len(before) :]
    rows = z_t_ref.shape[1]
    for ref, held in zip((soft_ref, own_ref, acc_ref), before or (None,) * 3):
        ref[...] = jnp.zeros_like(ref) if first else held[...]

    @pl.loop(0, raw_ref.shape[0] // tile)
    def _(index):
        here = pl.ds(pl.multiple_of(index * tile, tile), tile)
        c = normalize_rows(raw_ref[here])[0].astype(bf16)
        exponent = jnp.exp(dot(c, z_t_ref[...], 1, 0) * sharpness)
        acc_ref[...] += jnp.sum(exponent.reshape(-1, 8, rows), axis=0)
        exponent = exponent.astype(bf16)
        exp_ref[here] = exponent
        soft_ref[...] += dot(c, exponent, 0, 0)
        own_ref[...] += dot(code_columns(code_ref, columns_ref, group, index, unit), c, 1, 0)

    if last:
        totals = jnp.sum(acc_ref[...], axis=0, keepdims=True)
        for r in range(rows // 128):
            lanes = jnp.broadcast_to(totals[:, r * 128 : (r + 1) * 128], (total_ref.shape[0], 128))
            total_ref[:, r] = lanes
    else:
        total_ref[...] = acc_ref[...]


def prototypes_kernel(
    columns_ref, totals_ref, z_t_ref, local_ref, incoming_ref, code_ref, exp_ref, out_ref, zw_ref,
    *, group, unit, crops, own_images
):
    weights = row_weights(totals_ref, crops, own_images)
    zw_ref[...] = (z_t_ref[...].astype(f32) * weights).astype(bf16)
    target = (local_ref[...] + incoming_ref[...]).astype(bf16)

    @pl.loop(0, exp_ref.shape[0] // tile)
    def _(index):
        here = pl.ds(pl.multiple_of(index * tile, tile), tile)
        code = code_columns(code_ref, columns_ref, group, index, unit)
        grads = dot(exp_ref[here], zw_ref[...], 1, 1) - dot(code, target, 0, 0)
        out_ref[here] = grads * grad_scale


def rows_kernel(totals_ref, soft_ref, own_ref, out_ref, *, crops, own_images):
    weights = row_weights(totals_ref, crops, own_images)
    own_rows = crops * own_images
    n_proto = out_ref.shape[0]
    features = out_ref.shape[2]
    soft = (soft_ref[...] * weights).T
    out_ref[:, :own_rows] = soft.reshape(n_proto, own_rows, features)
    out_ref[:, own_rows:] = own_ref[...].reshape(n_proto, own_images, features)


def finish_kernel(total_ref, raw_ref, out_ref):
    unit_proto, length = normalize_rows(raw_ref[...])
    grad = total_ref[...] * (1.0 / grad_scale)
    along = jnp.sum(unit_proto * grad, axis=-1, keepdims=True)
    out_ref[...] = (grad - unit_proto * along) / length


def shape(*dims, dtype=f32):
    return jax.ShapeDtypeStruct(dims, dtype)


def call(kernel, out_shape, operands, mib=12, scalars=False, scratch=()):
    kept = pl.BlockSpec(memory_space=pltpu.VMEM)
    specs = [kept] * len(operands)
    if scalars:
        specs[0] = pl.BlockSpec(memory_space=pltpu.SMEM)
    return pl.pallas_call(
        kernel,
        out_shape=out_shape,
        in_specs=specs,
        out_specs=jax.tree.map(lambda _: kept, out_shape),
        scratch_shapes=scratch,
        compiler_params=pltpu.CompilerParams(vmem_limit_bytes=mib << 20),
    )(*operands)


def on_device(embeddings, codes, prototypes):
    n_proto = lax.axis_size("proto")
    own_images, _, crops, features = embeddings.shape
    images = own_images * n_proto
    rows = images * crops
    own_rows = own_images * crops
    code = codes[:, 0]
    unit = prototypes.shape[1]

    place = lax.axis_index(owners)
    near, far = jnp.arange(side), jnp.arange(side)[:, None]
    columns = (place ^ (near * side) ^ far).reshape(-1).astype(jnp.int32)

    column = {0: prototypes[0]}
    for j in (1, 3, 2):
        column[j] = exchange(prototypes[0], "y", j)

    by_crop = jnp.swapaxes(embeddings[:, 0], 0, 1)
    own_emb = by_crop.reshape(1, own_rows, features)
    raw_emb = lax.all_to_all(
        jnp.broadcast_to(own_emb, (n_proto, own_rows, features)), "proto", 0, 0
    )

    gathered = {0: jnp.concatenate([column[j] for j in range(side)])}
    for d in arrivals:
        gathered[d] = exchange(gathered[0], "x", d)

    z_t, local_sum, outgoing = call(
        embeddings_kernel,
        (shape(features, rows, dtype=bf16), shape(images, features), shape(images, features)),
        (raw_emb.reshape(n_proto, crops, own_images, features),),
    )

    exponents = {}
    state = ()
    for d in (0, *arrivals):
        last = d == arrivals[-1]
        total_dims = (n_proto, rows // 128, 128) if last else (8, rows)
        exponents[d], *state = call(
            functools.partial(scores_kernel, group=d, unit=unit, first=not state, last=last),
            [
                shape(side * unit, rows, dtype=bf16),
                shape(features, rows),
                shape(images, features),
                shape(*total_dims),
            ],
            (columns, z_t, code, *state, gathered[d]),
            scalars=True,
            scratch=[pltpu.VMEM((8, rows), f32)],
        )
    soft, own_term, totals, outgoing = lax.optimization_barrier((*state, outgoing))
    totals = lax.all_to_all(totals, "proto", 0, 0)
    incoming = swapped(outgoing)

    parts = {}
    for d in (*arrivals, 0):
        if d == 0:
            row_parts = call(
                functools.partial(rows_kernel, crops=crops, own_images=own_images),
                shape(n_proto, own_rows + own_images, features),
                (totals, soft, own_term),
            )
            row_parts = row_parts.astype(f16)
        parts[d] = call(
            functools.partial(
                prototypes_kernel, group=d, unit=unit, crops=crops, own_images=own_images
            ),
            shape(side * unit, features),
            (columns, totals, z_t, local_sum, incoming, code, exponents[d]),
            scalars=True,
            scratch=[pltpu.VMEM((features, rows), bf16)],
        )
        if d:
            parts[d] = parts[d].astype(f16)

    row_parts = lax.all_to_all(row_parts, "proto", 0, 0)

    column_sum = parts[0]
    for d in arrivals:
        column_sum = column_sum + exchange(parts[d], "x", d).astype(f32)
    column_sum = column_sum.reshape(side, unit, features)
    proto_sum = column_sum[0]
    for j in (1, 3, 2):
        part = exchange(column_sum[j].astype(f16), "y", j)
        proto_sum = proto_sum + part.astype(f32)

    row_sums = jnp.sum(row_parts.astype(f32), axis=0)
    own_code_term = row_sums[own_rows:]
    other_code_term = swapped(own_code_term)
    both = own_code_term + other_code_term
    assigned = jnp.stack([other_code_term] + [both] * (crops - 1))
    unit_emb, emb_norm = normalize_rows(by_crop)
    score_grad = (row_sums[:own_rows].reshape(crops, own_images, features) - assigned) * sharpness
    grad_emb = (
        score_grad - unit_emb * jnp.sum(unit_emb * score_grad, axis=-1, keepdims=True)
    ) / emb_norm
    grad_emb = jnp.swapaxes(grad_emb, 0, 1)[:, None]

    grad_proto = call(
        finish_kernel,
        shape(*prototypes.shape[1:]),
        (proto_sum, prototypes[0]),
    )
    return (grad_emb, grad_proto[None])


def solution(mesh):
    return jax.shard_map(
        on_device,
        mesh=mesh,
        in_specs=(
            P(("dp", "proto"), "crop", None, None),
            P("dp", "crop", "proto"),
            P("proto", ("dp", "crop"), None),
        ),
        out_specs=(P(("dp", "proto"), "crop", None, None), P("proto", ("dp", "crop"), None)),
        check_vma=False,
    )
```

```python
import functools

import jax
import jax.numpy as jnp
from jax import lax
from jax.experimental import pallas as pl
from jax.experimental.pallas import tpu as pltpu
from jax.sharding import PartitionSpec as P


sharpness = 10.0
epsilon = 1e-06
side = 4
near = (0, 1, 3, 2)
arrivals = (2, 1, 3)
kinds = (0, 1)
bf16, f32 = jnp.bfloat16, jnp.float32
owners = ("dp", "crop")


def swapped(value):
    return lax.ppermute(value, "crop", [(0, 1), (1, 0)])


def mask_of(axis, distance):
    return distance * side if axis == 0 else distance


def exchange(value, axis, distance):
    mask = mask_of(axis, distance)
    return lax.ppermute(value, owners, [(owner, owner ^ mask) for owner in range(side * side)])


def normalize_rows(values):
    floats = values.astype(f32)
    lengths = jnp.sqrt(jnp.sum(floats * floats, axis=-1, keepdims=True) + epsilon)
    return floats / lengths, lengths


def dot(left, right, left_dim, right_dim):
    return lax.dot_general(
        left, right, (((left_dim,), (right_dim,)), ((), ())), preferred_element_type=f32
    )


def row_weights(totals_ref, crops, own_images):
    totals = jnp.sum(totals_ref[...], axis=0)
    flat = jnp.concatenate([totals[r : r + 1] for r in range(totals.shape[0])], axis=1)
    lane = lax.broadcasted_iota(jnp.int32, flat.shape, 1)
    views = jnp.where((lane // own_images) % crops == 0, 1.0, 2.0).astype(f32)
    return views / flat


def code_columns(code_ref, kind, distance):
    place = lax.axis_index(owners)
    half = code_ref.shape[1] // (2 * side * side)
    parts = []
    for j in near:
        owner = place ^ (mask_of(kind, j) + mask_of(1 - kind, distance))
        first = pl.multiple_of((owner * 2 + kind) * half, half)
        parts.append(code_ref[:, pl.ds(first, half)])
    return jnp.concatenate(parts, axis=1)


def embeddings_kernel(raw_ref, z_t_ref, local_ref, outgoing_ref):
    z = normalize_rows(raw_ref[...])[0].astype(bf16).astype(f32)
    features = z.shape[-1]
    local = z[:, 1]
    for crop in range(2, z.shape[1]):
        local = local + z[:, crop]
    local_ref[...] = local.reshape(-1, features)
    outgoing_ref[...] = (z[:, 0] + local).reshape(-1, features)
    z_t_ref[...] = z.reshape(-1, features).T.astype(bf16)


def scores_kernel(*refs, distance, first, last):
    z_t_ref, code_ref = refs[:2]
    before = () if first else refs[2:5]
    refs = refs[2 + len(before) :]
    raw_refs, exp_refs, (soft_ref, own_ref, total_ref) = refs[:2], refs[2:4], refs[4:]
    rows = z_t_ref.shape[1]
    soft, own, acc = (None, None, None) if first else (ref[...] for ref in before)
    add = lambda a, b: b if a is None else a + b
    for kind in kinds:
        c = normalize_rows(raw_refs[kind][...])[0].astype(bf16)
        exponent = jnp.exp(dot(c, z_t_ref[...], 1, 0) * sharpness)
        acc = add(acc, jnp.sum(exponent.reshape(-1, 8, rows), axis=0))
        exponent = exponent.astype(bf16)
        exp_refs[kind][...] = exponent
        soft = add(soft, dot(c, exponent, 0, 0))
        own = add(own, dot(code_columns(code_ref, kind, distance), c, 1, 0))
    soft_ref[...] = soft
    own_ref[...] = own
    if last:
        totals = jnp.sum(acc, axis=0, keepdims=True)
        for r in range(rows // 128):
            lanes = jnp.broadcast_to(totals[:, r * 128 : (r + 1) * 128], (total_ref.shape[0], 128))
            total_ref[:, r] = lanes
    else:
        total_ref[...] = acc


def prototypes_kernel(
    totals_ref, z_t_ref, local_ref, incoming_ref, code_ref, exp_a_ref, exp_b_ref, *out_refs,
    distance, crops, own_images
):
    weights = row_weights(totals_ref, crops, own_images)
    zw = (z_t_ref[...].astype(f32) * weights).astype(bf16)
    target = (local_ref[...] + incoming_ref[...]).astype(bf16)
    for kind, exp_ref, out_ref in zip(kinds, (exp_a_ref, exp_b_ref), out_refs):
        code = code_columns(code_ref, kind, distance)
        grads = dot(exp_ref[...], zw, 1, 1) - dot(code, target, 0, 0)
        out_ref[...] = grads.astype(out_ref.dtype)


def rows_kernel(totals_ref, soft_ref, own_ref, other_ref, out_ref, *, crops, own_images):
    weights = row_weights(totals_ref, crops, own_images)
    n_proto = out_ref.shape[0]
    features = out_ref.shape[3]
    soft = (soft_ref[...] * weights).T.reshape(n_proto, crops, own_images, features)
    own = own_ref[...].reshape(n_proto, own_images, features)
    other = other_ref[...].reshape(n_proto, own_images, features)
    for crop in range(crops):
        assigned = other if crop == 0 else own + other
        out_ref[:, crop] = ((soft[:, crop] - assigned) * sharpness).astype(bf16)


def finish_rows_kernel(parts_ref, raw_ref, out_ref):
    score_grad = jnp.sum(parts_ref[...].astype(f32), axis=0)
    unit, length = normalize_rows(raw_ref[...])
    grad = (score_grad - unit * jnp.sum(unit * score_grad, axis=-1, keepdims=True)) / length
    for crop in range(grad.shape[0]):
        out_ref[:, crop] = grad[crop]


def far_sum_kernel(held_ref, *refs):
    parts, (keep_ref, send_ref) = refs[:-2], refs[-2:]
    total = held_ref[...]
    for part in parts:
        total = total + part[...].astype(f32)
    half = total.shape[0] // 2
    keep_ref[...] = total[:half]
    send_ref[...] = total[half:].astype(bf16)


def near_sum_kernel(held_ref, part_ref, keep_ref, send_ref):
    total = held_ref[...] + part_ref[...].astype(f32)
    half = total.shape[0] // 2
    keep_ref[...] = total[:half]
    send_ref[...] = total[half:].astype(bf16)


def finish_kernel(held_a_ref, part_a_ref, held_b_ref, part_b_ref, raw_ref, out_ref):
    half = held_a_ref.shape[0]
    for kind, held, part in ((0, held_a_ref, part_a_ref), (1, held_b_ref, part_b_ref)):
        here = pl.ds(kind * half, half)
        grad = held[...] + part[...].astype(f32)
        unit, length = normalize_rows(raw_ref[here])
        along = jnp.sum(unit * grad, axis=-1, keepdims=True)
        out_ref[here] = (grad - unit * along) / length


def shape(*dims, dtype=f32):
    return jax.ShapeDtypeStruct(dims, dtype)


def call(kernel, out_shape, *operands, mib=12):
    kept = pl.BlockSpec(memory_space=pltpu.VMEM)
    return pl.pallas_call(
        kernel,
        out_shape=out_shape,
        in_specs=[kept] * len(operands),
        out_specs=jax.tree.map(lambda _: kept, out_shape),
        compiler_params=pltpu.CompilerParams(vmem_limit_bytes=mib << 20),
    )(*operands)


def on_device(embeddings, codes, prototypes):
    n_proto = lax.axis_size("proto")
    own_images, _, crops, features = embeddings.shape
    images = own_images * n_proto
    rows = images * crops
    own_rows = own_images * crops
    code = codes[:, 0]
    half = prototypes.shape[1] // 2

    by_crop = jnp.swapaxes(embeddings[:, 0], 0, 1)
    halves = [prototypes[0, :half], prototypes[0, half:]]
    for step, distance in enumerate((1, 3)):
        moved = []
        for kind in kinds:
            moved.append(exchange(halves[kind], kind, distance))
        halves = [jnp.concatenate(pair) for pair in zip(halves, moved)]
        if step == 0:
            own_emb = by_crop.reshape(1, own_rows, features)
            raw_emb = lax.all_to_all(
                jnp.broadcast_to(own_emb, (n_proto, own_rows, features)), "proto", 0, 0
            )
    gathered = {0: halves}
    for d in arrivals:
        gathered[d] = []
        for kind in kinds:
            gathered[d].append(exchange(halves[kind], 1 - kind, d))

    z_t, local_sum, outgoing = call(
        embeddings_kernel,
        (shape(features, rows, dtype=bf16), shape(images, features), shape(images, features)),
        raw_emb.reshape(n_proto, crops, own_images, features),
    )

    exponents = {}
    state = ()
    for d in (0, *arrivals):
        last = d == arrivals[-1]
        total_dims = (n_proto, rows // 128, 128) if last else (8, rows)
        *exponents[d], soft, own_term, totals = call(
            functools.partial(scores_kernel, distance=d, first=not state, last=last),
            [shape(side * half, rows, dtype=bf16)] * 2
            + [shape(features, rows), shape(images, features), shape(*total_dims)],
            z_t, code, *state, *gathered[d],
        )
        state = (soft, own_term, totals)
    totals, outgoing = lax.optimization_barrier((totals, outgoing))
    incoming = swapped(outgoing)
    totals = lax.all_to_all(totals, "proto", 0, 0)
    own_term, totals = lax.optimization_barrier((own_term, totals))
    other_term = swapped(own_term)

    arrived = [[], []]
    for d in (*arrivals, 0):
        parts = call(
            functools.partial(prototypes_kernel, distance=d, crops=crops, own_images=own_images),
            [shape(side * half, features, dtype=bf16 if d else f32)] * 2,
            totals, z_t, local_sum, incoming, code, *exponents[d],
        )
        for kind in kinds:
            if d:
                arrived[kind].append(exchange(parts[kind], 1 - kind, d))
            else:
                arrived[kind].insert(0, parts[kind])

    row_parts = call(
        functools.partial(rows_kernel, crops=crops, own_images=own_images),
        shape(n_proto, crops, own_images, features, dtype=bf16),
        totals, soft, own_term, other_term,
    )
    row_parts = lax.all_to_all(row_parts, "proto", 0, 0)

    held = []
    for kind in kinds:
        keep, send = call(
            far_sum_kernel,
            [shape(2 * half, features), shape(2 * half, features, dtype=bf16)],
            *arrived[kind],
        )
        held.append((keep, exchange(send, kind, 3)))
    operands = []
    for kind, (keep, part) in zip(kinds, held):
        keep, send = call(
            near_sum_kernel,
            [shape(half, features), shape(half, features, dtype=bf16)],
            keep, part,
        )
        operands += [keep, exchange(send, kind, 1)]
    grad_proto = call(finish_kernel, shape(*prototypes.shape[1:]), *operands, prototypes[0])

    grad_emb = call(finish_rows_kernel, shape(own_images, crops, features), row_parts, by_crop)
    return (grad_emb[:, None], grad_proto[None])


def solution(mesh):
    return jax.shard_map(
        on_device,
        mesh=mesh,
        in_specs=(
            P(("dp", "proto"), "crop", None, None),
            P("dp", "crop", "proto"),
            P("proto", ("dp", "crop"), None),
        ),
        out_specs=(P(("dp", "proto"), "crop", None, None), P("proto", ("dp", "crop"), None)),
        check_vma=False,
    )
```

```python
import functools

import jax
import jax.numpy as jnp
from jax import lax
from jax.experimental import pallas as pl
from jax.experimental.pallas import tpu as pltpu
from jax.sharding import PartitionSpec as P


sharpness = 10.0
epsilon = 1e-06
side = 4
near = (0, 1, 3, 2)
arrivals = (2, 1, 3)
kinds = (0, 1)
bf16, f32 = jnp.bfloat16, jnp.float32
owners = ("dp", "crop")


def swapped(value):
    return lax.ppermute(value, "crop", [(0, 1), (1, 0)])


def mask_of(axis, distance):
    return distance * side if axis == 0 else distance


def exchange(value, axis, distance):
    mask = mask_of(axis, distance)
    return lax.ppermute(value, owners, [(owner, owner ^ mask) for owner in range(side * side)])


def normalize_rows(values):
    floats = values.astype(f32)
    lengths = jnp.sqrt(jnp.sum(floats * floats, axis=-1, keepdims=True) + epsilon)
    return floats / lengths, lengths


def dot(left, right, left_dim, right_dim):
    return lax.dot_general(
        left, right, (((left_dim,), (right_dim,)), ((), ())), preferred_element_type=f32
    )


def row_weights(totals_ref, crops, own_images):
    totals = jnp.sum(totals_ref[...], axis=0)
    flat = jnp.concatenate([totals[r : r + 1] for r in range(totals.shape[0])], axis=1)
    lane = lax.broadcasted_iota(jnp.int32, flat.shape, 1)
    views = jnp.where((lane // own_images) % crops == 0, 1.0, 2.0).astype(f32)
    return views / flat


def code_columns(code_ref, kind, distance):
    place = lax.axis_index(owners)
    half = code_ref.shape[1] // (2 * side * side)
    parts = []
    for j in near:
        owner = place ^ (mask_of(kind, j) + mask_of(1 - kind, distance))
        first = pl.multiple_of((owner * 2 + kind) * half, half)
        parts.append(code_ref[:, pl.ds(first, half)])
    return jnp.concatenate(parts, axis=1)


def split_kernel(proto_ref, emb_ref, first_ref, second_ref, own_ref, spread_ref):
    half = first_ref.shape[0]
    first_ref[...] = proto_ref[:half]
    second_ref[...] = proto_ref[half:]
    emb = emb_ref[...].astype(f32)
    own = jnp.concatenate([emb[:, crop] for crop in range(emb.shape[1])]).astype(bf16)
    own_ref[...] = own.reshape(own_ref.shape)
    for peer in range(spread_ref.shape[0]):
        spread_ref[peer] = own


def embeddings_kernel(raw_ref, z_t_ref, local_ref, outgoing_ref):
    z = normalize_rows(raw_ref[...])[0].astype(bf16).astype(f32)
    features = z.shape[-1]
    local = z[:, 1]
    for crop in range(2, z.shape[1]):
        local = local + z[:, crop]
    local_ref[...] = local.reshape(-1, features)
    outgoing_ref[...] = (z[:, 0] + local).reshape(-1, features)
    z_t_ref[...] = z.reshape(-1, features).T.astype(bf16)


def scores_kernel(*refs, distance, first, last):
    z_t_ref, code_ref = refs[:2]
    before = () if first else refs[2:5]
    refs = refs[2 + len(before) :]
    raw_refs, exp_refs, (soft_ref, own_ref, total_ref) = refs[:2], refs[2:4], refs[4:]
    rows = z_t_ref.shape[1]
    soft, own, acc = (None, None, None) if first else (ref[...] for ref in before)
    add = lambda a, b: b if a is None else a + b
    for kind in kinds:
        c = normalize_rows(raw_refs[kind][...])[0].astype(bf16)
        exponent = jnp.exp(dot(c, z_t_ref[...], 1, 0) * sharpness)
        acc = add(acc, jnp.sum(exponent.reshape(-1, 8, rows), axis=0))
        exponent = exponent.astype(bf16)
        exp_refs[kind][...] = exponent
        soft = add(soft, dot(c, exponent, 0, 0))
        own = add(own, dot(code_columns(code_ref, kind, distance), c, 1, 0))
    soft_ref[...] = soft
    own_ref[...] = own
    if last:
        totals = jnp.sum(acc, axis=0, keepdims=True)
        for r in range(rows // 128):
            lanes = jnp.broadcast_to(totals[:, r * 128 : (r + 1) * 128], (total_ref.shape[0], 128))
            total_ref[:, r] = lanes
    else:
        total_ref[...] = acc


def prototypes_kernel(*refs, distance, crops, own_images, first):
    if first:
        totals_ref, z_t_ref, local_ref, incoming_ref = refs[:4]
        weights = row_weights(totals_ref, crops, own_images)
        zw = (z_t_ref[...].astype(f32) * weights).astype(bf16)
        target = (local_ref[...] + incoming_ref[...]).astype(bf16)
        refs[-2][...] = zw
        refs[-1][...] = target
        refs = refs[4:-2]
    else:
        zw, target = refs[0][...], refs[1][...]
        refs = refs[2:]
    code_ref, exp_a_ref, exp_b_ref, *out_refs = refs
    for kind, exp_ref, out_ref in zip(kinds, (exp_a_ref, exp_b_ref), out_refs):
        code = code_columns(code_ref, kind, distance)
        grads = dot(exp_ref[...], zw, 1, 1) - dot(code, target, 0, 0)
        out_ref[...] = grads.astype(out_ref.dtype)


def rows_kernel(totals_ref, soft_ref, own_ref, other_ref, out_ref, *, crops, own_images):
    weights = row_weights(totals_ref, crops, own_images)
    n_proto = out_ref.shape[0]
    features = out_ref.shape[3]
    soft = (soft_ref[...] * weights).T.reshape(n_proto, crops, own_images, features)
    own = own_ref[...].reshape(n_proto, own_images, features)
    other = other_ref[...].reshape(n_proto, own_images, features)
    for crop in range(crops):
        assigned = other if crop == 0 else own + other
        out_ref[:, crop] = ((soft[:, crop] - assigned) * sharpness).astype(bf16)


def finish_rows_kernel(parts_ref, raw_ref, out_ref):
    score_grad = jnp.sum(parts_ref[...].astype(f32), axis=0)
    unit, length = normalize_rows(raw_ref[...])
    grad = (score_grad - unit * jnp.sum(unit * score_grad, axis=-1, keepdims=True)) / length
    for crop in range(grad.shape[0]):
        out_ref[:, crop] = grad[crop]


def far_sum_kernel(held_ref, *refs):
    parts, (keep_ref, send_ref) = refs[:-2], refs[-2:]
    total = held_ref[...]
    for part in parts:
        total = total + part[...].astype(f32)
    half = total.shape[0] // 2
    keep_ref[...] = total[:half]
    send_ref[...] = total[half:].astype(bf16)


def near_sum_kernel(held_ref, part_ref, keep_ref, send_ref):
    total = held_ref[...] + part_ref[...].astype(f32)
    half = total.shape[0] // 2
    keep_ref[...] = total[:half]
    send_ref[...] = total[half:].astype(bf16)


def finish_kernel(held_a_ref, part_a_ref, held_b_ref, part_b_ref, raw_ref, out_ref):
    half = held_a_ref.shape[0]
    for kind, held, part in ((0, held_a_ref, part_a_ref), (1, held_b_ref, part_b_ref)):
        here = pl.ds(kind * half, half)
        grad = held[...] + part[...].astype(f32)
        unit, length = normalize_rows(raw_ref[here])
        along = jnp.sum(unit * grad, axis=-1, keepdims=True)
        out_ref[here] = (grad - unit * along) / length


def shape(*dims, dtype=f32):
    return jax.ShapeDtypeStruct(dims, dtype)


def call(kernel, out_shape, *operands, mib=12):
    kept = pl.BlockSpec(memory_space=pltpu.VMEM)
    return pl.pallas_call(
        kernel,
        out_shape=out_shape,
        in_specs=[kept] * len(operands),
        out_specs=jax.tree.map(lambda _: kept, out_shape),
        compiler_params=pltpu.CompilerParams(vmem_limit_bytes=mib << 20),
    )(*operands)


def on_device(embeddings, codes, prototypes):
    n_proto = lax.axis_size("proto")
    own_images, _, crops, features = embeddings.shape
    images = own_images * n_proto
    rows = images * crops
    own_rows = own_images * crops
    code = codes[:, 0]
    half = prototypes.shape[1] // 2

    *halves, by_crop, spread_emb = call(
        split_kernel,
        [
            shape(half, features, dtype=bf16),
            shape(half, features, dtype=bf16),
            shape(crops, own_images, features, dtype=bf16),
            shape(n_proto, own_rows, features, dtype=bf16),
        ],
        prototypes[0], embeddings[:, 0],
    )
    for step, distance in enumerate((1, 3)):
        moved = []
        for kind in kinds:
            moved.append(exchange(halves[kind], kind, distance))
        halves = [jnp.concatenate(pair) for pair in zip(halves, moved)]
        if step == 0:
            raw_emb = lax.all_to_all(spread_emb, "proto", 0, 0)
    gathered = {0: halves}
    for d in arrivals:
        gathered[d] = []
        for kind in kinds:
            gathered[d].append(exchange(halves[kind], 1 - kind, d))

    z_t, local_sum, outgoing = call(
        embeddings_kernel,
        (shape(features, rows, dtype=bf16), shape(images, features), shape(images, features)),
        raw_emb.reshape(n_proto, crops, own_images, features),
    )

    exponents = {}
    state = ()
    for d in (0, *arrivals):
        last = d == arrivals[-1]
        total_dims = (n_proto, rows // 128, 128) if last else (8, rows)
        *exponents[d], soft, own_term, totals = call(
            functools.partial(scores_kernel, distance=d, first=not state, last=last),
            [shape(side * half, rows, dtype=bf16)] * 2
            + [shape(features, rows), shape(images, features), shape(*total_dims)],
            z_t, code, *state, *gathered[d],
        )
        state = (soft, own_term, totals)
    totals, outgoing = lax.optimization_barrier((totals, outgoing))
    incoming = swapped(outgoing)
    other_term = swapped(own_term)
    totals = lax.all_to_all(totals, "proto", 0, 0)

    arrived = [[], []]
    for d in (*arrivals, 0):
        first = d == arrivals[0]
        outs = call(
            functools.partial(
                prototypes_kernel,
                distance=d, crops=crops, own_images=own_images, first=first,
            ),
            [shape(side * half, features, dtype=bf16 if d else f32)] * 2
            + [shape(features, rows, dtype=bf16), shape(images, features, dtype=bf16)] * first,
            *((totals, z_t, local_sum, incoming) if first else (zw, target)),
            code, *exponents[d],
        )
        parts = outs[:2]
        if first:
            zw, target = outs[2:]
        for kind in kinds:
            if d:
                arrived[kind].append(exchange(parts[kind], 1 - kind, d))
            else:
                arrived[kind].insert(0, parts[kind])

    held_parts = [arrived[kind][0] for kind in kinds]
    soft, *held_parts = lax.optimization_barrier((soft, *held_parts))
    for kind in kinds:
        arrived[kind][0] = held_parts[kind]
    row_parts = call(
        functools.partial(rows_kernel, crops=crops, own_images=own_images),
        shape(n_proto, crops, own_images, features, dtype=bf16),
        totals, soft, own_term, other_term,
    )
    row_parts = lax.all_to_all(row_parts, "proto", 0, 0)

    held = []
    for kind in kinds:
        keep, send = call(
            far_sum_kernel,
            [shape(2 * half, features), shape(2 * half, features, dtype=bf16)],
            *arrived[kind],
        )
        held.append((keep, exchange(send, kind, 3)))
    operands = []
    for kind, (keep, part) in zip(kinds, held):
        keep, send = call(
            near_sum_kernel,
            [shape(half, features), shape(half, features, dtype=bf16)],
            keep, part,
        )
        operands += [keep, exchange(send, kind, 1)]
    grad_proto = call(finish_kernel, shape(*prototypes.shape[1:]), *operands, prototypes[0])

    grad_emb = call(
        finish_rows_kernel, shape(own_images, crops, features), row_parts, by_crop
    )
    return (grad_emb[:, None], grad_proto[None])


def solution(mesh):
    return jax.shard_map(
        on_device,
        mesh=mesh,
        in_specs=(
            P(("dp", "proto"), "crop", None, None),
            P("dp", "crop", "proto"),
            P("proto", ("dp", "crop"), None),
        ),
        out_specs=(P(("dp", "proto"), "crop", None, None), P("proto", ("dp", "crop"), None)),
        check_vma=False,
    )
```

```python
import functools

import jax
import jax.numpy as jnp
from jax import lax
from jax.experimental import pallas as pl
from jax.experimental.pallas import tpu as pltpu
from jax.sharding import PartitionSpec as P


sharpness = 10.0
epsilon = 1e-06
side = 4
near = (0, 1, 3, 2)
arrivals = (2, 1, 3)
kinds = (0, 1)
bf16, f32 = jnp.bfloat16, jnp.float32
owners = ("dp", "crop")


def swapped(value):
    return lax.ppermute(value, "crop", [(0, 1), (1, 0)])


def mask_of(axis, distance):
    return distance * side if axis == 0 else distance


def exchange(value, axis, distance):
    mask = mask_of(axis, distance)
    return lax.ppermute(value, owners, [(owner, owner ^ mask) for owner in range(side * side)])


def normalize_rows(values):
    floats = values.astype(f32)
    lengths = jnp.sqrt(jnp.sum(floats * floats, axis=-1, keepdims=True) + epsilon)
    return floats / lengths, lengths


def dot(left, right, left_dim, right_dim):
    return lax.dot_general(
        left, right, (((left_dim,), (right_dim,)), ((), ())), preferred_element_type=f32
    )


def row_weights(totals_ref, crops, own_images):
    totals = jnp.sum(totals_ref[...], axis=0)
    flat = jnp.concatenate([totals[r : r + 1] for r in range(totals.shape[0])], axis=1)
    lane = lax.broadcasted_iota(jnp.int32, flat.shape, 1)
    views = jnp.where((lane // own_images) % crops == 0, 1.0, 2.0).astype(f32)
    return views / flat


def code_columns(code_ref, kind, distance):
    place = lax.axis_index(owners)
    half = code_ref.shape[1] // (2 * side * side)
    parts = []
    for j in near:
        owner = place ^ (mask_of(kind, j) + mask_of(1 - kind, distance))
        first = pl.multiple_of((owner * 2 + kind) * half, half)
        parts.append(code_ref[:, pl.ds(first, half)])
    return jnp.concatenate(parts, axis=1)


def split_kernel(
    proto_ref, emb_ref, first_ref, second_ref, own_ref, spread_ref, proto_buf, emb_buf, sem_a, sem_b
):
    proto_copy, emb_copy = fetch((proto_ref, emb_ref), (proto_buf, emb_buf), (sem_a, sem_b))
    half = first_ref.shape[0]
    proto_copy.wait()
    first_ref[...] = proto_buf[:half]
    second_ref[...] = proto_buf[half:]
    emb_copy.wait()
    emb = emb_buf[...].astype(f32)
    own = jnp.concatenate([emb[:, crop] for crop in range(emb.shape[1])]).astype(bf16)
    own_ref[...] = own.reshape(own_ref.shape)
    for peer in range(spread_ref.shape[0]):
        spread_ref[peer] = own


def embeddings_kernel(raw_ref, z_t_ref, local_ref, outgoing_ref):
    z = normalize_rows(raw_ref[...])[0].astype(bf16).astype(f32)
    features = z.shape[-1]
    local = z[:, 1]
    for crop in range(2, z.shape[1]):
        local = local + z[:, crop]
    local_ref[...] = local.reshape(-1, features)
    outgoing_ref[...] = (z[:, 0] + local).reshape(-1, features)
    z_t_ref[...] = z.reshape(-1, features).T.astype(bf16)


def scores_kernel(*refs, distance, n_before):
    z_t_ref, code_ref, *raw_refs = refs[:4]
    own_before, acc_before = refs[4 : 4 + n_before], refs[4 + n_before : 4 + 2 * n_before]
    exp_a_ref, exp_b_ref, soft_ref, own_ref, total_ref = refs[4 + 2 * n_before : 9 + 2 * n_before]
    raw_bufs, copies = raw_refs, ()
    if distance:
        raw_bufs, semaphores = refs[-4:-2], refs[-2:]
        copies = fetch(raw_refs, raw_bufs, semaphores)
    rows = z_t_ref.shape[1]
    soft = own = acc = None
    add = lambda a, b: b if a is None else a + b
    for kind, exp_ref in zip(kinds, (exp_a_ref, exp_b_ref)):
        if copies:
            copies[kind].wait()
        c = normalize_rows(raw_bufs[kind][...])[0].astype(bf16)
        exponent = jnp.exp(dot(c, z_t_ref[...], 1, 0) * sharpness)
        acc = add(acc, jnp.sum(exponent.reshape(-1, 8, rows), axis=0))
        exponent = exponent.astype(bf16)
        exp_ref[...] = exponent
        soft = add(soft, dot(c, exponent, 0, 0))
        own = add(own, dot(code_columns(code_ref, kind, distance), c, 1, 0))
    soft_ref[...] = soft
    for before in own_before:
        own = own + before[...]
    own_ref[...] = own
    if not n_before:
        total_ref[...] = acc
        return
    for before in acc_before:
        acc = acc + before[...]
    totals = jnp.sum(acc, axis=0, keepdims=True)
    for r in range(rows // 128):
        lanes = jnp.broadcast_to(totals[:, r * 128 : (r + 1) * 128], (total_ref.shape[0], 128))
        total_ref[:, r] = lanes


def prototypes_kernel(*refs, distance, crops, own_images, first):
    if first:
        totals_ref, z_t_ref, local_ref, incoming_ref = refs[:4]
        weights = row_weights(totals_ref, crops, own_images)
        zw = (z_t_ref[...].astype(f32) * weights).astype(bf16)
        target = (local_ref[...] + incoming_ref[...]).astype(bf16)
        refs[-2][...] = zw
        refs[-1][...] = target
        refs = refs[4:-2]
    else:
        zw, target = refs[0][...], refs[1][...]
        refs = refs[2:]
    code_ref, exp_a_ref, exp_b_ref, *out_refs = refs
    for kind, exp_ref, out_ref in zip(kinds, (exp_a_ref, exp_b_ref), out_refs):
        code = code_columns(code_ref, kind, distance)
        grads = dot(exp_ref[...], zw, 1, 1) - dot(code, target, 0, 0)
        out_ref[...] = grads.astype(out_ref.dtype)


def rows_kernel(totals_ref, own_ref, other_ref, *refs, crops, own_images):
    *soft_refs, out_ref = refs
    soft_sum = sum(ref[...] for ref in soft_refs[1:]) + soft_refs[0][...]
    weights = row_weights(totals_ref, crops, own_images)
    n_proto = out_ref.shape[0]
    features = out_ref.shape[3]
    soft = (soft_sum * weights).T.reshape(n_proto, crops, own_images, features)
    own = own_ref[...].reshape(n_proto, own_images, features)
    other = other_ref[...].reshape(n_proto, own_images, features)
    for crop in range(crops):
        assigned = other if crop == 0 else own + other
        out_ref[:, crop] = ((soft[:, crop] - assigned) * sharpness).astype(bf16)


def finish_rows_kernel(parts_ref, raw_ref, out_ref):
    score_grad = jnp.sum(parts_ref[...].astype(f32), axis=0)
    unit, length = normalize_rows(raw_ref[...])
    grad = (score_grad - unit * jnp.sum(unit * score_grad, axis=-1, keepdims=True)) / length
    for crop in range(grad.shape[0]):
        out_ref[:, crop] = grad[crop]


def far_sum_kernel(held_ref, *refs):
    n = len(arrivals)
    sources, (keep_ref, send_ref), refs = refs[:n], refs[n : n + 2], refs[n + 2 :]
    buffers, semaphores = refs[:n], refs[n:]
    copies = fetch(sources, buffers, semaphores)
    total = held_ref[...]
    for copy, buffer in zip(copies, buffers):
        copy.wait()
        total = total + buffer[...].astype(f32)
    half = total.shape[0] // 2
    keep_ref[...] = total[:half]
    send_ref[...] = total[half:].astype(bf16)


def near_sum_kernel(held_ref, part_ref, keep_ref, send_ref):
    total = held_ref[...] + part_ref[...].astype(f32)
    half = total.shape[0] // 2
    keep_ref[...] = total[:half]
    send_ref[...] = total[half:].astype(bf16)


def finish_kernel(held_a_ref, part_a_ref, held_b_ref, part_b_ref, raw_ref, out_ref):
    half = held_a_ref.shape[0]
    for kind, held, part in ((0, held_a_ref, part_a_ref), (1, held_b_ref, part_b_ref)):
        here = pl.ds(kind * half, half)
        grad = held[...] + part[...].astype(f32)
        unit, length = normalize_rows(raw_ref[here])
        along = jnp.sum(unit * grad, axis=-1, keepdims=True)
        out_ref[here] = (grad - unit * along) / length


def shape(*dims, dtype=f32):
    return jax.ShapeDtypeStruct(dims, dtype)


def call(kernel, out_shape, *operands, mib=12, fetched=(), scratch=()):
    kept = pl.BlockSpec(memory_space=pltpu.VMEM)
    there = pl.BlockSpec(memory_space=pl.ANY)
    return pl.pallas_call(
        kernel,
        out_shape=out_shape,
        in_specs=[there if i in fetched else kept for i in range(len(operands))],
        out_specs=jax.tree.map(lambda _: kept, out_shape),
        scratch_shapes=[
            *(pltpu.VMEM(operands[i].shape, operands[i].dtype) for i in fetched),
            *(pltpu.SemaphoreType.DMA(()) for _ in fetched),
            *scratch,
        ],
        compiler_params=pltpu.CompilerParams(vmem_limit_bytes=mib << 20),
    )(*operands)


def fetch(sources, buffers, semaphores):
    copies = [pltpu.make_async_copy(*each) for each in zip(sources, buffers, semaphores)]
    for copy in copies:
        copy.start()
    return copies


def on_device(embeddings, codes, prototypes):
    n_proto = lax.axis_size("proto")
    own_images, _, crops, features = embeddings.shape
    images = own_images * n_proto
    rows = images * crops
    own_rows = own_images * crops
    code = codes[:, 0]
    half = prototypes.shape[1] // 2

    *halves, by_crop, spread_emb = call(
        split_kernel,
        [
            shape(half, features, dtype=bf16),
            shape(half, features, dtype=bf16),
            shape(crops, own_images, features, dtype=bf16),
            shape(n_proto, own_rows, features, dtype=bf16),
        ],
        *(pltpu.with_memory_space_constraint(x, pltpu.HBM) for x in (prototypes[0], embeddings[:, 0])),
        fetched=(0, 1),
    )
    blocks = [[halves[kind]] for kind in kinds]
    for j in near[1:]:
        for kind in kinds:
            blocks[kind].append(exchange(halves[kind], kind, j))
    halves = [jnp.concatenate(each) for each in blocks]
    raw_emb = lax.all_to_all(spread_emb, "proto", 0, 0)
    gathered = {0: halves}
    for d in arrivals:
        gathered[d] = []
        for kind in kinds:
            gathered[d].append(exchange(halves[kind], 1 - kind, d))

    z_t, local_sum, outgoing = call(
        embeddings_kernel,
        (shape(features, rows, dtype=bf16), shape(images, features), shape(images, features)),
        raw_emb.reshape(n_proto, crops, own_images, features),
    )

    exponents = {}
    soft, own_sums, sums = [], [], []
    for d in (0, *arrivals):
        before = (*own_sums, *sums) if d == arrivals[-1] else ()
        total_dims = (n_proto, rows // 128, 128) if before else (8, rows)
        *exponents[d], soft_part, own_term, totals = call(
            functools.partial(scores_kernel, distance=d, n_before=len(before) // 2),
            [shape(side * half, rows, dtype=bf16)] * 2
            + [shape(features, rows), shape(images, features), shape(*total_dims)],
            z_t, code, *gathered[d], *before,
            fetched=(2, 3) if d else (),
        )
        soft.append(soft_part)
        own_sums.append(own_term)
        sums.append(totals)
    totals, outgoing = lax.optimization_barrier((totals, outgoing))
    incoming = swapped(outgoing)
    other_term = swapped(own_term)
    totals = lax.all_to_all(totals, "proto", 0, 0)

    arrived = [[], []]
    for d in (*arrivals, 0):
        first = d == arrivals[0]
        outs = call(
            functools.partial(
                prototypes_kernel,
                distance=d, crops=crops, own_images=own_images, first=first,
            ),
            [shape(side * half, features, dtype=bf16 if d else f32)] * 2
            + [shape(features, rows, dtype=bf16), shape(images, features, dtype=bf16)] * first,
            *((totals, z_t, local_sum, incoming) if first else (zw, target)),
            code, *exponents[d],
        )
        parts = outs[:2]
        if first:
            zw, target = outs[2:]
        for kind in kinds:
            if d:
                arrived[kind].append(exchange(parts[kind], 1 - kind, d))
            else:
                arrived[kind].insert(0, parts[kind])

    held_parts = [arrived[kind][0] for kind in kinds]
    soft[0], *held_parts = lax.optimization_barrier((soft[0], *held_parts))
    for kind in kinds:
        arrived[kind][0] = held_parts[kind]
    row_parts = call(
        functools.partial(rows_kernel, crops=crops, own_images=own_images),
        shape(n_proto, crops, own_images, features, dtype=bf16),
        totals, own_term, other_term, *soft,
    )
    row_parts = lax.all_to_all(row_parts, "proto", 0, 0)

    held = []
    for kind in kinds:
        keep, send = call(
            far_sum_kernel,
            [shape(2 * half, features), shape(2 * half, features, dtype=bf16)],
            *arrived[kind],
            fetched=tuple(range(1, len(arrived[kind]))),
        )
        held.append((keep, exchange(send, kind, 3)))
    operands = []
    for kind, (keep, part) in zip(kinds, held):
        keep, send = call(
            near_sum_kernel,
            [shape(half, features), shape(half, features, dtype=bf16)],
            keep, part,
        )
        operands += [keep, exchange(send, kind, 1)]
    grad_proto = call(finish_kernel, shape(*prototypes.shape[1:]), *operands, prototypes[0])

    grad_emb = call(
        finish_rows_kernel, shape(own_images, crops, features), row_parts, by_crop
    )
    return (grad_emb[:, None], grad_proto[None])


def solution(mesh):
    return jax.shard_map(
        on_device,
        mesh=mesh,
        in_specs=(
            P(("dp", "proto"), "crop", None, None),
            P("dp", "crop", "proto"),
            P("proto", ("dp", "crop"), None),
        ),
        out_specs=(P(("dp", "proto"), "crop", None, None), P("proto", ("dp", "crop"), None)),
        check_vma=False,
    )
```

```python
import functools

import jax
import jax.numpy as jnp
from jax import lax
from jax.experimental import pallas as pl
from jax.experimental.pallas import tpu as pltpu
from jax.sharding import PartitionSpec as P


sharpness = 10.0
epsilon = 1e-06
side = 4
near = (0, 1, 3, 2)
arrivals = (2, 1, 3)
kinds = (0, 1)
bf16, f32 = jnp.bfloat16, jnp.float32
owners = ("dp", "crop")


def swapped(value):
    return lax.ppermute(value, "crop", [(0, 1), (1, 0)])


def mask_of(axis, distance):
    return distance * side if axis == 0 else distance


def exchange(value, axis, distance):
    mask = mask_of(axis, distance)
    return lax.ppermute(value, owners, [(owner, owner ^ mask) for owner in range(side * side)])


def normalize_rows(values):
    floats = values.astype(f32)
    lengths = jnp.sqrt(jnp.sum(floats * floats, axis=-1, keepdims=True) + epsilon)
    return floats / lengths, lengths


def dot(left, right, left_dim, right_dim):
    return lax.dot_general(
        left, right, (((left_dim,), (right_dim,)), ((), ())), preferred_element_type=f32
    )


def row_weights(totals_ref, crops, own_images):
    totals = jnp.sum(totals_ref[...], axis=0)
    flat = jnp.concatenate([totals[r : r + 1] for r in range(totals.shape[0])], axis=1)
    lane = lax.broadcasted_iota(jnp.int32, flat.shape, 1)
    views = jnp.where((lane // own_images) % crops == 0, 1.0, 2.0).astype(f32)
    return views / flat


def fetch_codes(code_ref, buffer, semaphores, distance):
    place = lax.axis_index(owners)
    half = code_ref.shape[1] // (2 * side * side)
    copies = [[], []]
    for kind in kinds:
        for index, j in enumerate(near):
            owner = place ^ (mask_of(kind, j) + mask_of(1 - kind, distance))
            first = pl.multiple_of((owner * 2 + kind) * half, half)
            copy = pltpu.make_async_copy(
                code_ref.at[:, pl.ds(first, half)],
                buffer.at[kind, :, pl.ds(index * half, half)],
                semaphores.at[kind * side + index],
            )
            copy.start()
            copies[kind].append(copy)
    return copies


def fetched_code(copies, buffer, kind):
    for copy in copies[kind]:
        copy.wait()
    return buffer[kind]


def split_kernel(
    proto_ref, emb_ref, first_ref, second_ref, own_ref, spread_ref, proto_buf, emb_buf, sem_a, sem_b
):
    proto_copy, emb_copy = fetch((proto_ref, emb_ref), (proto_buf, emb_buf), (sem_a, sem_b))
    half = first_ref.shape[0]
    proto_copy.wait()
    first_ref[...] = proto_buf[:half]
    second_ref[...] = proto_buf[half:]
    emb_copy.wait()
    emb = emb_buf[...].astype(f32)
    own = jnp.concatenate([emb[:, crop] for crop in range(emb.shape[1])]).astype(bf16)
    own_ref[...] = own.reshape(own_ref.shape)
    for peer in range(spread_ref.shape[0]):
        spread_ref[peer] = own


def embeddings_kernel(raw_ref, z_t_ref, local_ref, outgoing_ref):
    z = normalize_rows(raw_ref[...])[0].astype(bf16).astype(f32)
    features = z.shape[-1]
    local = z[:, 1]
    for crop in range(2, z.shape[1]):
        local = local + z[:, crop]
    local_ref[...] = local.reshape(-1, features)
    outgoing_ref[...] = (z[:, 0] + local).reshape(-1, features)
    z_t_ref[...] = z.reshape(-1, features).T.astype(bf16)


def scores_kernel(*refs, distance, n_before):
    z_t_ref, code_ref, *raw_refs = refs[:4]
    own_before, acc_before = refs[4 : 4 + n_before], refs[4 + n_before : 4 + 2 * n_before]
    exp_a_ref, exp_b_ref, soft_ref, own_ref, total_ref = refs[4 + 2 * n_before : 9 + 2 * n_before]
    code_buf, semaphores = refs[-2:]
    copies = fetch_codes(code_ref, code_buf, semaphores, distance)
    rows = z_t_ref.shape[1]
    soft = own = acc = None
    add = lambda a, b: b if a is None else a + b
    for kind, exp_ref in zip(kinds, (exp_a_ref, exp_b_ref)):
        c = normalize_rows(raw_refs[kind][...])[0].astype(bf16)
        exponent = jnp.exp(dot(c, z_t_ref[...], 1, 0) * sharpness)
        acc = add(acc, jnp.sum(exponent.reshape(-1, 8, rows), axis=0))
        exponent = exponent.astype(bf16)
        exp_ref[...] = exponent
        soft = add(soft, dot(c, exponent, 0, 0))
        own = add(own, dot(fetched_code(copies, code_buf, kind), c, 1, 0))
    soft_ref[...] = soft
    for before in own_before:
        own = own + before[...]
    own_ref[...] = own
    if not n_before:
        total_ref[...] = acc
        return
    for before in acc_before:
        acc = acc + before[...]
    totals = jnp.sum(acc, axis=0, keepdims=True)
    for r in range(rows // 128):
        lanes = jnp.broadcast_to(totals[:, r * 128 : (r + 1) * 128], (total_ref.shape[0], 128))
        total_ref[:, r] = lanes


def prototypes_kernel(*refs, distance, crops, own_images, first):
    *refs, code_buf, semaphores = refs
    code_ref, *refs = refs
    copies = fetch_codes(code_ref, code_buf, semaphores, distance)
    if first:
        totals_ref, z_t_ref, local_ref, incoming_ref = refs[:4]
        weights = row_weights(totals_ref, crops, own_images)
        zw = (z_t_ref[...].astype(f32) * weights).astype(bf16)
        target = (local_ref[...] + incoming_ref[...]).astype(bf16)
        refs[-2][...] = zw
        refs[-1][...] = target
        refs = refs[4:-2]
    else:
        zw, target = refs[0][...], refs[1][...]
        refs = refs[2:]
    exp_a_ref, exp_b_ref, *out_refs = refs
    for kind, exp_ref, out_ref in zip(kinds, (exp_a_ref, exp_b_ref), out_refs):
        grads = dot(exp_ref[...], zw, 1, 1)
        grads = grads - dot(fetched_code(copies, code_buf, kind), target, 0, 0)
        out_ref[...] = grads.astype(out_ref.dtype)


def rows_kernel(totals_ref, own_ref, other_ref, *refs, crops, own_images):
    *soft_refs, out_ref = refs
    soft_sum = sum(ref[...] for ref in soft_refs[1:]) + soft_refs[0][...]
    weights = row_weights(totals_ref, crops, own_images)
    n_proto = out_ref.shape[0]
    features = out_ref.shape[3]
    soft = (soft_sum * weights).T.reshape(n_proto, crops, own_images, features)
    own = own_ref[...].reshape(n_proto, own_images, features)
    other = other_ref[...].reshape(n_proto, own_images, features)
    for crop in range(crops):
        assigned = other if crop == 0 else own + other
        out_ref[:, crop] = ((soft[:, crop] - assigned) * sharpness).astype(bf16)


def finish_rows_kernel(parts_ref, raw_ref, out_ref):
    score_grad = jnp.sum(parts_ref[...].astype(f32), axis=0)
    unit, length = normalize_rows(raw_ref[...])
    grad = (score_grad - unit * jnp.sum(unit * score_grad, axis=-1, keepdims=True)) / length
    for crop in range(grad.shape[0]):
        out_ref[:, crop] = grad[crop]


def far_sum_kernel(held_ref, *refs):
    parts, (keep_ref, send_ref) = refs[:-2], refs[-2:]
    total = held_ref[...]
    for part in parts:
        total = total + part[...].astype(f32)
    half = total.shape[0] // 2
    keep_ref[...] = total[:half]
    send_ref[...] = total[half:].astype(bf16)


def near_sum_kernel(held_ref, part_ref, keep_ref, send_ref):
    total = held_ref[...] + part_ref[...].astype(f32)
    half = total.shape[0] // 2
    keep_ref[...] = total[:half]
    send_ref[...] = total[half:].astype(bf16)


def finish_kernel(held_a_ref, part_a_ref, held_b_ref, part_b_ref, raw_ref, out_ref):
    half = held_a_ref.shape[0]
    for kind, held, part in ((0, held_a_ref, part_a_ref), (1, held_b_ref, part_b_ref)):
        here = pl.ds(kind * half, half)
        grad = held[...] + part[...].astype(f32)
        unit, length = normalize_rows(raw_ref[here])
        along = jnp.sum(unit * grad, axis=-1, keepdims=True)
        out_ref[here] = (grad - unit * along) / length


def shape(*dims, dtype=f32):
    return jax.ShapeDtypeStruct(dims, dtype)


def call(kernel, out_shape, *operands, mib=12, fetched=(), held=(), scratch=()):
    operands = [
        pltpu.with_memory_space_constraint(x, pltpu.HBM) if i in held else x
        for i, x in enumerate(operands)
    ]
    kept = pl.BlockSpec(memory_space=pltpu.VMEM)
    there = pl.BlockSpec(memory_space=pl.ANY)
    return pl.pallas_call(
        kernel,
        out_shape=out_shape,
        in_specs=[there if i in (*fetched, *held) else kept for i in range(len(operands))],
        out_specs=jax.tree.map(lambda _: kept, out_shape),
        scratch_shapes=[
            *(pltpu.VMEM(operands[i].shape, operands[i].dtype) for i in fetched),
            *(pltpu.SemaphoreType.DMA(()) for _ in fetched),
            *scratch,
        ],
        compiler_params=pltpu.CompilerParams(vmem_limit_bytes=mib << 20),
    )(*operands)


def fetch(sources, buffers, semaphores):
    copies = [pltpu.make_async_copy(*each) for each in zip(sources, buffers, semaphores)]
    for copy in copies:
        copy.start()
    return copies


def on_device(embeddings, codes, prototypes):
    n_proto = lax.axis_size("proto")
    own_images, _, crops, features = embeddings.shape
    images = own_images * n_proto
    rows = images * crops
    own_rows = own_images * crops
    code = codes[:, 0]
    half = prototypes.shape[1] // 2

    *halves, by_crop, spread_emb = call(
        split_kernel,
        [
            shape(half, features, dtype=bf16),
            shape(half, features, dtype=bf16),
            shape(crops, own_images, features, dtype=bf16),
            shape(n_proto, own_rows, features, dtype=bf16),
        ],
        prototypes[0], embeddings[:, 0],
        fetched=(0, 1), held=(0, 1),
    )
    for step, distance in enumerate((1, 3)):
        moved = []
        for kind in kinds:
            moved.append(exchange(halves[kind], kind, distance))
        halves = [jnp.concatenate(pair) for pair in zip(halves, moved)]
        if step == 0:
            raw_emb = lax.all_to_all(spread_emb, "proto", 0, 0)
    gathered = {0: halves}
    for d in arrivals:
        gathered[d] = []
        for kind in kinds:
            gathered[d].append(exchange(halves[kind], 1 - kind, d))

    z_t, local_sum, outgoing = call(
        embeddings_kernel,
        (shape(features, rows, dtype=bf16), shape(images, features), shape(images, features)),
        raw_emb.reshape(n_proto, crops, own_images, features),
    )

    code_scratch = [
        pltpu.VMEM((2, images, side * half), bf16),
        pltpu.SemaphoreType.DMA((2 * side,)),
    ]
    exponents = {}
    soft, own_sums, sums = [], [], []
    for d in (0, *arrivals):
        before = (*own_sums, *sums) if d == arrivals[-1] else ()
        total_dims = (n_proto, rows // 128, 128) if before else (8, rows)
        *exponents[d], soft_part, own_term, totals = call(
            functools.partial(scores_kernel, distance=d, n_before=len(before) // 2),
            [shape(side * half, rows, dtype=bf16)] * 2
            + [shape(features, rows), shape(images, features), shape(*total_dims)],
            z_t, code, *gathered[d], *before,
            held=(1,),
            scratch=code_scratch,
        )
        soft.append(soft_part)
        own_sums.append(own_term)
        sums.append(totals)
    totals, outgoing = lax.optimization_barrier((totals, outgoing))
    incoming = swapped(outgoing)
    other_term = swapped(own_term)
    totals = lax.all_to_all(totals, "proto", 0, 0)

    arrived = [[], []]
    for d in (*arrivals, 0):
        first = d == arrivals[0]
        outs = call(
            functools.partial(
                prototypes_kernel,
                distance=d, crops=crops, own_images=own_images, first=first,
            ),
            [shape(side * half, features, dtype=bf16 if d else f32)] * 2
            + [shape(features, rows, dtype=bf16), shape(images, features, dtype=bf16)] * first,
            code, *((totals, z_t, local_sum, incoming) if first else (zw, target)),
            *exponents[d],
            held=(0,),
            scratch=code_scratch,
        )
        parts = outs[:2]
        if first:
            zw, target = outs[2:]
        for kind in kinds:
            if d:
                arrived[kind].append(exchange(parts[kind], 1 - kind, d))
            else:
                arrived[kind].insert(0, parts[kind])

    held_parts = [arrived[kind][0] for kind in kinds]
    soft[0], *held_parts = lax.optimization_barrier((soft[0], *held_parts))
    for kind in kinds:
        arrived[kind][0] = held_parts[kind]
    row_parts = call(
        functools.partial(rows_kernel, crops=crops, own_images=own_images),
        shape(n_proto, crops, own_images, features, dtype=bf16),
        totals, own_term, other_term, *soft,
    )
    row_parts = lax.all_to_all(row_parts, "proto", 0, 0)

    held = []
    for kind in kinds:
        keep, send = call(
            far_sum_kernel,
            [shape(2 * half, features), shape(2 * half, features, dtype=bf16)],
            *arrived[kind],
        )
        held.append((keep, exchange(send, kind, 3)))
    operands = []
    for kind, (keep, part) in zip(kinds, held):
        keep, send = call(
            near_sum_kernel,
            [shape(half, features), shape(half, features, dtype=bf16)],
            keep, part,
        )
        operands += [keep, exchange(send, kind, 1)]
    grad_proto = call(finish_kernel, shape(*prototypes.shape[1:]), *operands, prototypes[0])

    grad_emb = call(
        finish_rows_kernel, shape(own_images, crops, features), row_parts, by_crop
    )
    return (grad_emb[:, None], grad_proto[None])


def solution(mesh):
    return jax.shard_map(
        on_device,
        mesh=mesh,
        in_specs=(
            P(("dp", "proto"), "crop", None, None),
            P("dp", "crop", "proto"),
            P("proto", ("dp", "crop"), None),
        ),
        out_specs=(P(("dp", "proto"), "crop", None, None), P("proto", ("dp", "crop"), None)),
        check_vma=False,
    )
```

```python
import functools

import jax
import jax.numpy as jnp
from jax import lax
from jax.experimental import pallas as pl
from jax.experimental.pallas import tpu as pltpu
from jax.sharding import Mesh, PartitionSpec as P


sharpness = 10.0
epsilon = 1e-06
side = 4
near = (0, 1, 3, 2)
arrivals = (2, 1, 3)
kinds = (0, 1)
bf16, f32 = jnp.bfloat16, jnp.float32
owners = ("dp", "crop")
block = ("z", "core")


def swapped(value):
    return lax.ppermute(value, "crop", [(0, 1), (1, 0)])


def mask_of(axis, distance):
    return distance * side if axis == 0 else distance


def exchange(value, axis, distance):
    mask = mask_of(axis, distance)
    return lax.ppermute(value, owners, [(owner, owner ^ mask) for owner in range(side * side)])


def normalize_rows(values):
    floats = values.astype(f32)
    lengths = jnp.sqrt(jnp.sum(floats * floats, axis=-1, keepdims=True) + epsilon)
    return floats / lengths, lengths


def dot(left, right, left_dim, right_dim):
    return lax.dot_general(
        left, right, (((left_dim,), (right_dim,)), ((), ())), preferred_element_type=f32
    )


def row_weights(totals_ref, crops, own_images):
    totals = jnp.sum(totals_ref[...], axis=0)
    flat = jnp.concatenate([totals[r : r + 1] for r in range(totals.shape[0])], axis=1)
    lane = lax.broadcasted_iota(jnp.int32, flat.shape, 1)
    views = jnp.where((lane // own_images) % crops == 0, 1.0, 2.0).astype(f32)
    return views / flat


def code_columns(code_ref, kind, distance):
    place = lax.axis_index(owners)
    half = code_ref.shape[1] // (2 * side * side)
    parts = []
    for j in near:
        owner = place ^ (mask_of(kind, j) + mask_of(1 - kind, distance))
        first = pl.multiple_of((owner * 2 + kind) * half, half)
        parts.append(code_ref[:, pl.ds(first, half)])
    return jnp.concatenate(parts, axis=1)


def split_kernel(
    proto_ref, emb_ref, first_ref, second_ref, own_ref, spread_ref, proto_buf, emb_buf, sem_a, sem_b
):
    proto_copy, emb_copy = fetch((proto_ref, emb_ref), (proto_buf, emb_buf), (sem_a, sem_b))
    half = first_ref.shape[0]
    proto_copy.wait()
    first_ref[...] = proto_buf[:half]
    second_ref[...] = proto_buf[half:]
    emb_copy.wait()
    emb = emb_buf[...].astype(f32)
    own = jnp.concatenate([emb[:, crop] for crop in range(emb.shape[1])]).astype(bf16)
    own_ref[...] = own.reshape(own_ref.shape)
    for peer in range(spread_ref.shape[0]):
        spread_ref[peer] = own


def embeddings_kernel(code_ref, raw_ref, z_t_ref, local_ref, outgoing_ref, near_code_ref, semaphores):
    n = semaphores.shape[0]
    step = code_ref.shape[0] // n
    copies = []
    for index in range(n):
        here = pl.ds(index * step, step)
        copies.append(
            pltpu.make_async_copy(code_ref.at[here], near_code_ref.at[here], semaphores.at[index])
        )
        copies[-1].start()
    z = normalize_rows(raw_ref[...])[0].astype(bf16).astype(f32)
    features = z.shape[-1]
    local = z[:, 1]
    for crop in range(2, z.shape[1]):
        local = local + z[:, crop]
    local_ref[...] = local.reshape(-1, features)
    outgoing_ref[...] = (z[:, 0] + local).reshape(-1, features)
    z_t_ref[...] = z.reshape(-1, features).T.astype(bf16)
    for copy in copies:
        copy.wait()


def scores_kernel(*refs, distance, n_before):
    z_t_ref, code_ref, *raw_refs = refs[:4]
    own_before, acc_before = refs[4 : 4 + n_before], refs[4 + n_before : 4 + 2 * n_before]
    exp_a_ref, exp_b_ref, soft_ref, own_ref, total_ref = refs[4 + 2 * n_before : 9 + 2 * n_before]
    rows = z_t_ref.shape[1]
    soft = own = acc = None
    add = lambda a, b: b if a is None else a + b
    for kind, exp_ref in zip(kinds, (exp_a_ref, exp_b_ref)):
        c = normalize_rows(raw_refs[kind][...])[0].astype(bf16)
        exponent = jnp.exp(dot(c, z_t_ref[...], 1, 0) * sharpness)
        acc = add(acc, jnp.sum(exponent.reshape(-1, 8, rows), axis=0))
        exponent = exponent.astype(bf16)
        exp_ref[...] = exponent
        soft = add(soft, dot(c, exponent, 0, 0))
        own = add(own, dot(code_columns(code_ref, kind, distance), c, 1, 0))
    soft_ref[...] = soft
    for before in own_before:
        own = own + before[...]
    own_ref[...] = own
    if not n_before:
        total_ref[...] = acc
        return
    for before in acc_before:
        acc = acc + before[...]
    totals = jnp.sum(acc, axis=0, keepdims=True)
    for r in range(rows // 128):
        lanes = jnp.broadcast_to(totals[:, r * 128 : (r + 1) * 128], (total_ref.shape[0], 128))
        total_ref[:, r] = lanes


def prototypes_kernel(*refs, distance, crops, own_images, first):
    code_ref, *refs = refs
    if first:
        totals_ref, z_t_ref, local_ref, incoming_ref = refs[:4]
        weights = row_weights(totals_ref, crops, own_images)
        zw = (z_t_ref[...].astype(f32) * weights).astype(bf16)
        target = (local_ref[...] + incoming_ref[...]).astype(bf16)
        refs[-2][...] = zw
        refs[-1][...] = target
        refs = refs[4:-2]
    else:
        zw, target = refs[0][...], refs[1][...]
        refs = refs[2:]
    exp_a_ref, exp_b_ref, *out_refs = refs
    for kind, exp_ref, out_ref in zip(kinds, (exp_a_ref, exp_b_ref), out_refs):
        grads = dot(exp_ref[...], zw, 1, 1)
        grads = grads - dot(code_columns(code_ref, kind, distance), target, 0, 0)
        out_ref[...] = grads.astype(out_ref.dtype)


def rows_kernel(totals_ref, own_ref, other_ref, *refs, crops, own_images):
    *soft_refs, kept_ref, sent_ref = refs
    soft = soft_refs[0][...]
    for ref in soft_refs[1:]:
        soft = soft + ref[...]
    weights = row_weights(totals_ref, crops, own_images)
    n_z, _, _, features = kept_ref.shape
    soft = (soft * weights).T.reshape(n_z, 2, crops, own_images, features)
    own = own_ref[...].reshape(n_z, 2, own_images, features)
    other = other_ref[...].reshape(n_z, 2, own_images, features)
    first = lax.axis_index("core") == 0
    for crop in range(crops):
        assigned = other if crop == 0 else own + other
        grads = (soft[:, :, crop] - assigned) * sharpness
        kept_ref[:, crop] = jnp.where(first, grads[:, 0], grads[:, 1])
        sent_ref[:, crop] = jnp.where(first, grads[:, 1], grads[:, 0]).astype(bf16)


def add_kernel(kept_ref, part_ref, out_ref):
    out_ref[...] = (kept_ref[...] + part_ref[...].astype(f32)).astype(bf16)


def finish_rows_kernel(parts_ref, raw_ref, out_ref):
    score_grad = jnp.sum(parts_ref[...].astype(f32), axis=0)
    unit, length = normalize_rows(raw_ref[...])
    grad = (score_grad - unit * jnp.sum(unit * score_grad, axis=-1, keepdims=True)) / length
    for crop in range(grad.shape[0]):
        out_ref[:, crop] = grad[crop]


def far_sum_kernel(held_ref, *refs):
    parts, (keep_ref, send_ref) = refs[:-2], refs[-2:]
    total = held_ref[...]
    for part in parts:
        total = total + part[...].astype(f32)
    half = total.shape[0] // 2
    keep_ref[...] = total[:half]
    send_ref[...] = total[half:].astype(bf16)


def near_sum_kernel(held_ref, part_ref, keep_ref, send_ref):
    total = held_ref[...] + part_ref[...].astype(f32)
    half = total.shape[0] // 2
    keep_ref[...] = total[:half]
    send_ref[...] = total[half:].astype(bf16)


def finish_kernel(held_a_ref, part_a_ref, held_b_ref, part_b_ref, raw_ref, out_ref):
    half = held_a_ref.shape[0]
    for kind, held, part in ((0, held_a_ref, part_a_ref), (1, held_b_ref, part_b_ref)):
        here = pl.ds(kind * half, half)
        grad = held[...] + part[...].astype(f32)
        unit, length = normalize_rows(raw_ref[here])
        along = jnp.sum(unit * grad, axis=-1, keepdims=True)
        out_ref[here] = (grad - unit * along) / length


def shape(*dims, dtype=f32):
    return jax.ShapeDtypeStruct(dims, dtype)


def call(kernel, out_shape, *operands, mib=12, fetched=(), held=(), scratch=()):
    operands = [
        pltpu.with_memory_space_constraint(x, pltpu.HBM) if i in held else x
        for i, x in enumerate(operands)
    ]
    kept = pl.BlockSpec(memory_space=pltpu.VMEM)
    there = pl.BlockSpec(memory_space=pl.ANY)
    return pl.pallas_call(
        kernel,
        out_shape=out_shape,
        in_specs=[there if i in (*fetched, *held) else kept for i in range(len(operands))],
        out_specs=jax.tree.map(lambda _: kept, out_shape, is_leaf=lambda x: hasattr(x, 'shape')),
        scratch_shapes=[
            *(pltpu.VMEM(operands[i].shape, operands[i].dtype) for i in fetched),
            *(pltpu.SemaphoreType.DMA(()) for _ in fetched),
            *scratch,
        ],
        compiler_params=pltpu.CompilerParams(vmem_limit_bytes=mib << 20),
    )(*operands)


def fetch(sources, buffers, semaphores):
    copies = [pltpu.make_async_copy(*each) for each in zip(sources, buffers, semaphores)]
    for copy in copies:
        copy.start()
    return copies


def on_device(embeddings, codes, prototypes):
    n_proto = lax.axis_size(block)
    own_images, _, crops, features = embeddings.shape
    images = own_images * n_proto
    rows = images * crops
    own_rows = own_images * crops
    code = codes[:, 0]
    half = prototypes.shape[1] // 2

    *halves, by_crop, spread_emb = call(
        split_kernel,
        [
            shape(half, features, dtype=bf16),
            shape(half, features, dtype=bf16),
            shape(crops, own_images, features, dtype=bf16),
            shape(n_proto, own_rows, features, dtype=bf16),
        ],
        prototypes[0], embeddings[:, 0],
        fetched=(0, 1), held=(0, 1),
    )
    for step, distance in enumerate((1, 3)):
        moved = []
        for kind in kinds:
            moved.append(exchange(halves[kind], kind, distance))
        halves = [jnp.concatenate(pair) for pair in zip(halves, moved)]
        if step == 0:
            raw_emb = lax.all_to_all(spread_emb, block, 0, 0)
    gathered = {0: halves}
    for d in arrivals:
        gathered[d] = []
        for kind in kinds:
            gathered[d].append(exchange(halves[kind], 1 - kind, d))

    z_t, local_sum, outgoing, code = call(
        embeddings_kernel,
        (
            shape(features, rows, dtype=bf16),
            shape(images, features),
            shape(images, features),
            pltpu.VMEM(code.shape, code.dtype),
        ),
        code, raw_emb.reshape(n_proto, crops, own_images, features),
        held=(0,),
        scratch=[pltpu.SemaphoreType.DMA((8,))],
    )

    exponents = {}
    soft, own_sums, sums = [], [], []
    for d in (0, *arrivals):
        before = (*own_sums, *sums) if d == arrivals[-1] else ()
        total_dims = (n_proto, rows // 128, 128) if before else (8, rows)
        *exponents[d], soft_part, own_term, totals = call(
            functools.partial(scores_kernel, distance=d, n_before=len(before) // 2),
            [shape(side * half, rows, dtype=bf16)] * 2
            + [shape(features, rows), shape(images, features), shape(*total_dims)],
            z_t, code, *gathered[d], *before,
        )
        soft.append(soft_part)
        own_sums.append(own_term)
        sums.append(totals)
    totals, outgoing = lax.optimization_barrier((totals, outgoing))
    incoming = swapped(outgoing)
    other_term = swapped(own_term)
    totals = lax.all_to_all(totals, block, 0, 0)

    arrived = [[], []]
    for d in (*arrivals, 0):
        first = d == arrivals[0]
        outs = call(
            functools.partial(
                prototypes_kernel,
                distance=d, crops=crops, own_images=own_images, first=first,
            ),
            [shape(side * half, features, dtype=bf16 if d else f32)] * 2
            + [shape(features, rows, dtype=bf16), shape(images, features, dtype=bf16)] * first,
            code, *((totals, z_t, local_sum, incoming) if first else (zw, target)),
            *exponents[d],
        )
        parts = outs[:2]
        if first:
            zw, target = outs[2:]
        for kind in kinds:
            if d:
                arrived[kind].append(exchange(parts[kind], 1 - kind, d))
            else:
                arrived[kind].insert(0, parts[kind])

    row_shape = (n_proto // 2, crops, own_images, features)
    kept_rows, sent_rows = call(
        functools.partial(rows_kernel, crops=crops, own_images=own_images),
        [shape(*row_shape), shape(*row_shape, dtype=bf16)],
        totals, own_term, other_term, *soft,
    )
    sent_rows = lax.ppermute(sent_rows, "core", [(0, 1), (1, 0)])
    held_parts = [arrived[kind][0] for kind in kinds]
    kept_rows, *held_parts = lax.optimization_barrier((kept_rows, *held_parts))
    for kind in kinds:
        arrived[kind][0] = held_parts[kind]
    row_parts = call(add_kernel, shape(*row_shape, dtype=bf16), kept_rows, sent_rows)
    row_parts = lax.all_to_all(row_parts, "z", 0, 0)

    held = []
    for kind in kinds:
        keep, send = call(
            far_sum_kernel,
            [shape(2 * half, features), shape(2 * half, features, dtype=bf16)],
            *arrived[kind],
        )
        held.append((keep, exchange(send, kind, 3)))
    operands = []
    for kind, (keep, part) in zip(kinds, held):
        keep, send = call(
            near_sum_kernel,
            [shape(half, features), shape(half, features, dtype=bf16)],
            keep, part,
        )
        operands += [keep, exchange(send, kind, 1)]
    grad_proto = call(finish_kernel, shape(*prototypes.shape[1:]), *operands, prototypes[0])

    grad_emb = call(
        finish_rows_kernel, shape(own_images, crops, features), row_parts, by_crop
    )
    return (grad_emb[:, None], grad_proto[None])


def solution(mesh):
    n_dp, n_proto, n_crop = mesh.devices.shape
    fine = Mesh(mesh.devices.reshape(n_dp, n_proto // 2, 2, n_crop), ("dp", *block, "crop"))
    return jax.shard_map(
        on_device,
        mesh=fine,
        in_specs=(
            P(("dp", *block), "crop", None, None),
            P("dp", "crop", block),
            P(block, ("dp", "crop"), None),
        ),
        out_specs=(P(("dp", *block), "crop", None, None), P(block, ("dp", "crop"), None)),
        check_vma=False,
    )
```

```python
import functools

import jax
import jax.numpy as jnp
from jax import lax
from jax.experimental import pallas as pl
from jax.experimental.pallas import tpu as pltpu
from jax.sharding import Mesh, PartitionSpec as P


sharpness = 10.0
epsilon = 1e-06
side = 4
near = (0, 1, 3, 2)
arrivals = (2, 1, 3)
kinds = (0, 1)
bf16, f32 = jnp.bfloat16, jnp.float32
owners = ("dp", "crop")
block = ("z", "core")


def swapped(value):
    return lax.ppermute(value, "crop", [(0, 1), (1, 0)])


def mask_of(axis, distance):
    return distance * side if axis == 0 else distance


def exchange(value, axis, distance):
    mask = mask_of(axis, distance)
    return lax.ppermute(value, owners, [(owner, owner ^ mask) for owner in range(side * side)])


def normalize_rows(values):
    floats = values.astype(f32)
    lengths = jnp.sqrt(jnp.sum(floats * floats, axis=-1, keepdims=True) + epsilon)
    return floats / lengths, lengths


def dot(left, right, left_dim, right_dim):
    return lax.dot_general(
        left, right, (((left_dim,), (right_dim,)), ((), ())), preferred_element_type=f32
    )


def row_weights(totals_ref, crops, own_images):
    totals = jnp.sum(totals_ref[...], axis=0)
    flat = jnp.concatenate([totals[r : r + 1] for r in range(totals.shape[0])], axis=1)
    lane = lax.broadcasted_iota(jnp.int32, flat.shape, 1)
    views = jnp.where((lane // own_images) % crops == 0, 1.0, 2.0).astype(f32)
    return views / flat


def code_columns(code_ref, kind, distance):
    place = lax.axis_index(owners)
    half = code_ref.shape[1] // (2 * side * side)
    parts = []
    for j in near:
        owner = place ^ (mask_of(kind, j) + mask_of(1 - kind, distance))
        first = pl.multiple_of((owner * 2 + kind) * half, half)
        parts.append(code_ref[:, pl.ds(first, half)])
    return jnp.concatenate(parts, axis=1)


def split_kernel(
    proto_ref, emb_ref, first_ref, second_ref, own_ref, spread_ref, proto_buf, emb_buf, sem_a, sem_b
):
    proto_copy, emb_copy = fetch((proto_ref, emb_ref), (proto_buf, emb_buf), (sem_a, sem_b))
    half = first_ref.shape[0]
    proto_copy.wait()
    first_ref[...] = proto_buf[:half]
    second_ref[...] = proto_buf[half:]
    emb_copy.wait()
    emb = emb_buf[...].astype(f32)
    own = jnp.concatenate([emb[:, crop] for crop in range(emb.shape[1])]).astype(bf16)
    own_ref[...] = own.reshape(own_ref.shape)
    for peer in range(spread_ref.shape[0]):
        spread_ref[peer] = own


def embeddings_kernel(
    code_ref, own_ref, other_ref, z_t_ref, local_ref, outgoing_ref, near_code_ref, semaphores
):
    n = semaphores.shape[0]
    step = code_ref.shape[0] // n
    copies = []
    for index in range(n):
        here = pl.ds(index * step, step)
        copies.append(
            pltpu.make_async_copy(code_ref.at[here], near_code_ref.at[here], semaphores.at[index])
        )
        copies[-1].start()
    first = lax.axis_index("core") == 0
    own, other = own_ref[...].astype(f32), other_ref[...].astype(f32)
    raw = jnp.stack([jnp.where(first, own, other), jnp.where(first, other, own)], axis=1)
    z = normalize_rows(raw.reshape(-1, *own.shape[1:]))[0].astype(bf16).astype(f32)
    features = z.shape[-1]
    local = z[:, 1]
    for crop in range(2, z.shape[1]):
        local = local + z[:, crop]
    local_ref[...] = local.reshape(-1, features)
    outgoing_ref[...] = (z[:, 0] + local).reshape(-1, features)
    z_t_ref[...] = z.reshape(-1, features).T.astype(bf16)
    for copy in copies:
        copy.wait()


def scores_kernel(*refs, distance, n_before):
    z_t_ref, code_ref, *raw_refs = refs[:4]
    own_before, acc_before = refs[4 : 4 + n_before], refs[4 + n_before : 4 + 2 * n_before]
    exp_a_ref, exp_b_ref, soft_ref, own_ref, total_ref = refs[4 + 2 * n_before : 9 + 2 * n_before]
    rows = z_t_ref.shape[1]
    soft = own = acc = None
    add = lambda a, b: b if a is None else a + b
    for kind, exp_ref in zip(kinds, (exp_a_ref, exp_b_ref)):
        c = normalize_rows(raw_refs[kind][...])[0].astype(bf16)
        exponent = jnp.exp(dot(c, z_t_ref[...], 1, 0) * sharpness)
        acc = add(acc, jnp.sum(exponent.reshape(-1, 8, rows), axis=0))
        exponent = exponent.astype(bf16)
        exp_ref[...] = exponent
        soft = add(soft, dot(c, exponent, 0, 0))
        own = add(own, dot(code_columns(code_ref, kind, distance), c, 1, 0))
    soft_ref[...] = soft
    for before in own_before:
        own = own + before[...]
    own_ref[...] = own
    if not n_before:
        total_ref[...] = acc
        return
    for before in acc_before:
        acc = acc + before[...]
    totals = jnp.sum(acc, axis=0, keepdims=True)
    for r in range(rows // 128):
        lanes = jnp.broadcast_to(totals[:, r * 128 : (r + 1) * 128], (total_ref.shape[0], 128))
        total_ref[:, r] = lanes


def prototypes_kernel(*refs, distance, crops, own_images, first):
    code_ref, *refs = refs
    if first:
        totals_ref, z_t_ref, local_ref, incoming_ref = refs[:4]
        weights = row_weights(totals_ref, crops, own_images)
        zw = (z_t_ref[...].astype(f32) * weights).astype(bf16)
        target = (local_ref[...] + incoming_ref[...]).astype(bf16)
        refs[-2][...] = zw
        refs[-1][...] = target
        refs = refs[4:-2]
    else:
        zw, target = refs[0][...], refs[1][...]
        refs = refs[2:]
    exp_a_ref, exp_b_ref, *out_refs = refs
    for kind, exp_ref, out_ref in zip(kinds, (exp_a_ref, exp_b_ref), out_refs):
        grads = dot(exp_ref[...], zw, 1, 1)
        grads = grads - dot(code_columns(code_ref, kind, distance), target, 0, 0)
        out_ref[...] = grads.astype(out_ref.dtype)


def rows_kernel(totals_ref, own_ref, other_ref, *refs, crops, own_images):
    *soft_refs, kept_ref, sent_ref = refs
    soft = soft_refs[0][...]
    for ref in soft_refs[1:]:
        soft = soft + ref[...]
    weights = row_weights(totals_ref, crops, own_images)
    n_z, _, _, features = kept_ref.shape
    soft = (soft * weights).T.reshape(n_z, 2, crops, own_images, features)
    own = own_ref[...].reshape(n_z, 2, own_images, features)
    other = other_ref[...].reshape(n_z, 2, own_images, features)
    first = lax.axis_index("core") == 0
    for crop in range(crops):
        assigned = other if crop == 0 else own + other
        grads = (soft[:, :, crop] - assigned) * sharpness
        kept_ref[:, crop] = jnp.where(first, grads[:, 0], grads[:, 1])
        sent_ref[:, crop] = jnp.where(first, grads[:, 1], grads[:, 0]).astype(bf16)


def add_kernel(kept_ref, part_ref, out_ref):
    out_ref[...] = (kept_ref[...] + part_ref[...].astype(f32)).astype(bf16)


def finish_rows_kernel(parts_ref, raw_ref, out_ref):
    score_grad = jnp.sum(parts_ref[...].astype(f32), axis=0)
    unit, length = normalize_rows(raw_ref[...])
    grad = (score_grad - unit * jnp.sum(unit * score_grad, axis=-1, keepdims=True)) / length
    for crop in range(grad.shape[0]):
        out_ref[:, crop] = grad[crop]


def far_sum_kernel(held_ref, *refs):
    parts, (keep_ref, send_ref) = refs[:-2], refs[-2:]
    total = held_ref[...]
    for part in parts:
        total = total + part[...].astype(f32)
    half = total.shape[0] // 2
    keep_ref[...] = total[:half]
    send_ref[...] = total[half:].astype(bf16)


def near_sum_kernel(held_ref, part_ref, keep_ref, send_ref):
    total = held_ref[...] + part_ref[...].astype(f32)
    half = total.shape[0] // 2
    keep_ref[...] = total[:half]
    send_ref[...] = total[half:].astype(bf16)


def finish_kernel(held_a_ref, part_a_ref, held_b_ref, part_b_ref, raw_ref, out_ref):
    half = held_a_ref.shape[0]
    for kind, held, part in ((0, held_a_ref, part_a_ref), (1, held_b_ref, part_b_ref)):
        here = pl.ds(kind * half, half)
        grad = held[...] + part[...].astype(f32)
        unit, length = normalize_rows(raw_ref[here])
        along = jnp.sum(unit * grad, axis=-1, keepdims=True)
        out_ref[here] = (grad - unit * along) / length


def shape(*dims, dtype=f32):
    return jax.ShapeDtypeStruct(dims, dtype)


def call(kernel, out_shape, *operands, mib=12, fetched=(), held=(), scratch=()):
    operands = [
        pltpu.with_memory_space_constraint(x, pltpu.HBM) if i in held else x
        for i, x in enumerate(operands)
    ]
    kept = pl.BlockSpec(memory_space=pltpu.VMEM)
    there = pl.BlockSpec(memory_space=pl.ANY)
    return pl.pallas_call(
        kernel,
        out_shape=out_shape,
        in_specs=[there if i in (*fetched, *held) else kept for i in range(len(operands))],
        out_specs=jax.tree.map(lambda _: kept, out_shape, is_leaf=lambda x: hasattr(x, 'shape')),
        scratch_shapes=[
            *(pltpu.VMEM(operands[i].shape, operands[i].dtype) for i in fetched),
            *(pltpu.SemaphoreType.DMA(()) for _ in fetched),
            *scratch,
        ],
        compiler_params=pltpu.CompilerParams(vmem_limit_bytes=mib << 20),
    )(*operands)


def fetch(sources, buffers, semaphores):
    copies = [pltpu.make_async_copy(*each) for each in zip(sources, buffers, semaphores)]
    for copy in copies:
        copy.start()
    return copies


def on_device(embeddings, codes, prototypes):
    n_proto = lax.axis_size(block)
    own_images, _, crops, features = embeddings.shape
    images = own_images * n_proto
    rows = images * crops
    own_rows = own_images * crops
    code = codes[:, 0]
    half = prototypes.shape[1] // 2

    *halves, by_crop, spread_emb = call(
        split_kernel,
        [
            shape(half, features, dtype=bf16),
            shape(half, features, dtype=bf16),
            shape(crops, own_images, features, dtype=bf16),
            shape(n_proto // 2, own_rows, features, dtype=bf16),
        ],
        prototypes[0], embeddings[:, 0],
        fetched=(0, 1), held=(0, 1),
    )
    for distance in (1, 3):
        moved = []
        for kind in kinds:
            moved.append(exchange(halves[kind], kind, distance))
        halves = [jnp.concatenate(pair) for pair in zip(halves, moved)]
    own_core = lax.all_to_all(spread_emb, "z", 0, 0)
    other_core = lax.ppermute(own_core, "core", [(0, 1), (1, 0)])
    gathered = {0: halves}
    for d in arrivals:
        gathered[d] = []
        for kind in kinds:
            gathered[d].append(exchange(halves[kind], 1 - kind, d))

    z_t, local_sum, outgoing, code = call(
        embeddings_kernel,
        (
            shape(features, rows, dtype=bf16),
            shape(images, features),
            shape(images, features),
            pltpu.VMEM(code.shape, code.dtype),
        ),
        code, *(
            each.reshape(n_proto // 2, crops, own_images, features)
            for each in (own_core, other_core)
        ),
        held=(0,),
        scratch=[pltpu.SemaphoreType.DMA((8,))],
    )

    exponents = {}
    soft, own_sums, sums = [], [], []
    for d in (0, *arrivals):
        before = (*own_sums, *sums) if d == arrivals[-1] else ()
        total_dims = (n_proto, rows // 128, 128) if before else (8, rows)
        *exponents[d], soft_part, own_term, totals = call(
            functools.partial(scores_kernel, distance=d, n_before=len(before) // 2),
            [shape(side * half, rows, dtype=bf16)] * 2
            + [shape(features, rows), shape(images, features), shape(*total_dims)],
            z_t, code, *gathered[d], *before,
        )
        soft.append(soft_part)
        own_sums.append(own_term)
        sums.append(totals)
    totals, outgoing = lax.optimization_barrier((totals, outgoing))
    incoming = swapped(outgoing)
    other_term = swapped(own_term)
    totals = lax.all_to_all(totals, block, 0, 0)

    arrived = [[], []]
    for d in (*arrivals, 0):
        first = d == arrivals[0]
        outs = call(
            functools.partial(
                prototypes_kernel,
                distance=d, crops=crops, own_images=own_images, first=first,
            ),
            [shape(side * half, features, dtype=bf16 if d else f32)] * 2
            + [shape(features, rows, dtype=bf16), shape(images, features, dtype=bf16)] * first,
            code, *((totals, z_t, local_sum, incoming) if first else (zw, target)),
            *exponents[d],
        )
        parts = outs[:2]
        if first:
            zw, target = outs[2:]
        for kind in kinds:
            if d:
                arrived[kind].append(exchange(parts[kind], 1 - kind, d))
            else:
                arrived[kind].insert(0, parts[kind])

    row_shape = (n_proto // 2, crops, own_images, features)
    kept_rows, sent_rows = call(
        functools.partial(rows_kernel, crops=crops, own_images=own_images),
        [shape(*row_shape), shape(*row_shape, dtype=bf16)],
        totals, own_term, other_term, *soft,
    )
    sent_rows = lax.ppermute(sent_rows, "core", [(0, 1), (1, 0)])
    held_parts = [arrived[kind][0] for kind in kinds]
    kept_rows, *held_parts = lax.optimization_barrier((kept_rows, *held_parts))
    for kind in kinds:
        arrived[kind][0] = held_parts[kind]
    row_parts = call(add_kernel, shape(*row_shape, dtype=bf16), kept_rows, sent_rows)
    row_parts = lax.all_to_all(row_parts, "z", 0, 0)

    held = []
    for kind in kinds:
        keep, send = call(
            far_sum_kernel,
            [shape(2 * half, features), shape(2 * half, features, dtype=bf16)],
            *arrived[kind],
        )
        held.append((keep, exchange(send, kind, 3)))
    operands = []
    for kind, (keep, part) in zip(kinds, held):
        keep, send = call(
            near_sum_kernel,
            [shape(half, features), shape(half, features, dtype=bf16)],
            keep, part,
        )
        operands += [keep, exchange(send, kind, 1)]
    grad_proto = call(finish_kernel, shape(*prototypes.shape[1:]), *operands, prototypes[0])

    grad_emb = call(
        finish_rows_kernel, shape(own_images, crops, features), row_parts, by_crop
    )
    return (grad_emb[:, None], grad_proto[None])


def solution(mesh):
    n_dp, n_proto, n_crop = mesh.devices.shape
    fine = Mesh(mesh.devices.reshape(n_dp, n_proto // 2, 2, n_crop), ("dp", *block, "crop"))
    return jax.shard_map(
        on_device,
        mesh=fine,
        in_specs=(
            P(("dp", *block), "crop", None, None),
            P("dp", "crop", block),
            P(block, ("dp", "crop"), None),
        ),
        out_specs=(P(("dp", *block), "crop", None, None), P(block, ("dp", "crop"), None)),
        check_vma=False,
    )
```

```python
import functools

import jax
import jax.numpy as jnp
from jax import lax
from jax.experimental import pallas as pl
from jax.experimental.pallas import tpu as pltpu
from jax.sharding import Mesh, PartitionSpec as P


sharpness = 10.0
epsilon = 1e-06
side = 4
near = (0, 1, 3, 2)
arrivals = (2, 1, 3)
kinds = (0, 1)
bf16, f32 = jnp.bfloat16, jnp.float32
owners = ("dp", "crop")
block = ("z", "core")


def swapped(value):
    return lax.ppermute(value, "crop", [(0, 1), (1, 0)])


def mask_of(axis, distance):
    return distance * side if axis == 0 else distance


def exchange(value, axis, distance):
    mask = mask_of(axis, distance)
    return lax.ppermute(value, owners, [(owner, owner ^ mask) for owner in range(side * side)])


def normalize_rows(values):
    floats = values.astype(f32)
    lengths = jnp.sqrt(jnp.sum(floats * floats, axis=-1, keepdims=True) + epsilon)
    return floats / lengths, lengths


def dot(left, right, left_dim, right_dim):
    return lax.dot_general(
        left, right, (((left_dim,), (right_dim,)), ((), ())), preferred_element_type=f32
    )


def row_weights(totals_ref, crops, own_images):
    totals = jnp.sum(totals_ref[...], axis=0)
    flat = jnp.concatenate([totals[r : r + 1] for r in range(totals.shape[0])], axis=1)
    lane = lax.broadcasted_iota(jnp.int32, flat.shape, 1)
    views = jnp.where((lane // own_images) % crops == 0, 1.0, 2.0).astype(f32)
    return views / flat


def code_columns(code_ref, kind, distance):
    place = lax.axis_index(owners)
    half = code_ref.shape[1] // (2 * side * side)
    parts = []
    for j in near:
        owner = place ^ (mask_of(kind, j) + mask_of(1 - kind, distance))
        first = pl.multiple_of((owner * 2 + kind) * half, half)
        parts.append(code_ref[:, pl.ds(first, half)])
    return jnp.concatenate(parts, axis=1)


def split_kernel(
    proto_ref, emb_ref, first_ref, second_ref, own_ref, spread_ref, proto_buf, emb_buf, sem_a, sem_b
):
    proto_copy, emb_copy = fetch((proto_ref, emb_ref), (proto_buf, emb_buf), (sem_a, sem_b))
    half = first_ref.shape[0]
    proto_copy.wait()
    first_ref[...] = proto_buf[:half]
    second_ref[...] = proto_buf[half:]
    emb_copy.wait()
    emb = emb_buf[...].astype(f32)
    own = jnp.concatenate([emb[:, crop] for crop in range(emb.shape[1])]).astype(bf16)
    own_ref[...] = own.reshape(own_ref.shape)
    for peer in range(spread_ref.shape[0]):
        spread_ref[peer] = own


def stage_kernel(code_ref, near_code_ref, semaphores):
    n = semaphores.shape[0]
    step = code_ref.shape[0] // n
    copies = []
    for index in range(n):
        here = pl.ds(index * step, step)
        copies.append(
            pltpu.make_async_copy(code_ref.at[here], near_code_ref.at[here], semaphores.at[index])
        )
        copies[-1].start()
    for copy in copies:
        copy.wait()


def embeddings_kernel(own_ref, other_ref, z_t_ref, local_ref, outgoing_ref):
    first = lax.axis_index("core") == 0
    own, other = own_ref[...].astype(f32), other_ref[...].astype(f32)
    raw = jnp.stack([jnp.where(first, own, other), jnp.where(first, other, own)], axis=1)
    z = normalize_rows(raw.reshape(-1, *own.shape[1:]))[0].astype(bf16).astype(f32)
    features = z.shape[-1]
    local = z[:, 1]
    for crop in range(2, z.shape[1]):
        local = local + z[:, crop]
    local_ref[...] = local.reshape(-1, features)
    outgoing_ref[...] = (z[:, 0] + local).reshape(-1, features)
    z_t_ref[...] = z.reshape(-1, features).T.astype(bf16)


def scores_kernel(*refs, distance, n_before):
    z_t_ref, code_ref, *raw_refs = refs[:4]
    own_before, acc_before = refs[4 : 4 + n_before], refs[4 + n_before : 4 + 2 * n_before]
    exp_a_ref, exp_b_ref, soft_ref, own_ref, total_ref = refs[-5:]
    rows = z_t_ref.shape[1]
    soft = own = acc = None
    add = lambda a, b: b if a is None else a + b
    for kind, exp_ref in zip(kinds, (exp_a_ref, exp_b_ref)):
        c = normalize_rows(raw_refs[kind][...])[0].astype(bf16)
        exponent = jnp.exp(dot(c, z_t_ref[...], 1, 0) * sharpness)
        acc = add(acc, jnp.sum(exponent.reshape(-1, 8, rows), axis=0))
        exponent = exponent.astype(bf16)
        exp_ref[...] = exponent
        soft = add(soft, dot(c, exponent, 0, 0))
        own = add(own, dot(code_columns(code_ref, kind, distance), c, 1, 0))
    soft_ref[...] = soft
    for before in own_before:
        own = own + before[...]
    if not n_before:
        own_ref[...] = own
        total_ref[...] = acc
        return
    own_ref[0] = own
    own_ref[1] = refs[4 + 2 * n_before][...]
    for before in acc_before:
        acc = acc + before[...]
    totals = jnp.sum(acc, axis=0, keepdims=True)
    for r in range(rows // 128):
        lanes = jnp.broadcast_to(totals[:, r * 128 : (r + 1) * 128], (total_ref.shape[0], 128))
        total_ref[:, r] = lanes


def prototypes_kernel(*refs, distance, crops, own_images, first):
    code_ref, *refs = refs
    if first:
        totals_ref, z_t_ref, local_ref, incoming_ref = refs[:4]
        weights = row_weights(totals_ref, crops, own_images)
        zw = (z_t_ref[...].astype(f32) * weights).astype(bf16)
        target = (local_ref[...] + incoming_ref[1]).astype(bf16)
        refs[-2][...] = zw
        refs[-1][...] = target
        refs = refs[4:-2]
    else:
        zw, target = refs[0][...], refs[1][...]
        refs = refs[2:]
    exp_a_ref, exp_b_ref, *out_refs = refs
    for kind, exp_ref, out_ref in zip(kinds, (exp_a_ref, exp_b_ref), out_refs):
        grads = dot(exp_ref[...], zw, 1, 1)
        grads = grads - dot(code_columns(code_ref, kind, distance), target, 0, 0)
        out_ref[...] = grads.astype(out_ref.dtype)


def rows_kernel(totals_ref, own_ref, other_ref, *refs, crops, own_images):
    *soft_refs, kept_ref, sent_ref = refs
    soft = soft_refs[0][...]
    for ref in soft_refs[1:]:
        soft = soft + ref[...]
    weights = row_weights(totals_ref, crops, own_images)
    n_z, _, _, features = kept_ref.shape
    soft = (soft * weights).T.reshape(n_z, 2, crops, own_images, features)
    own = own_ref[0].reshape(n_z, 2, own_images, features)
    other = other_ref[0].reshape(n_z, 2, own_images, features)
    first = lax.axis_index("core") == 0
    for crop in range(crops):
        assigned = other if crop == 0 else own + other
        grads = (soft[:, :, crop] - assigned) * sharpness
        kept_ref[:, crop] = jnp.where(first, grads[:, 0], grads[:, 1])
        sent_ref[:, crop] = jnp.where(first, grads[:, 1], grads[:, 0]).astype(bf16)


def add_kernel(kept_ref, part_ref, out_ref):
    out_ref[...] = (kept_ref[...] + part_ref[...].astype(f32)).astype(bf16)


def finish_rows_kernel(parts_ref, raw_ref, out_ref):
    score_grad = jnp.sum(parts_ref[...].astype(f32), axis=0)
    unit, length = normalize_rows(raw_ref[...])
    grad = (score_grad - unit * jnp.sum(unit * score_grad, axis=-1, keepdims=True)) / length
    for crop in range(grad.shape[0]):
        out_ref[:, crop] = grad[crop]


def far_sum_kernel(held_ref, *refs):
    parts, (keep_ref, send_ref) = refs[:-2], refs[-2:]
    total = held_ref[...]
    for part in parts:
        total = total + part[...].astype(f32)
    half = total.shape[0] // 2
    keep_ref[...] = total[:half]
    send_ref[...] = total[half:].astype(bf16)


def near_sum_kernel(held_ref, part_ref, keep_ref, send_ref):
    total = held_ref[...] + part_ref[...].astype(f32)
    half = total.shape[0] // 2
    keep_ref[...] = total[:half]
    send_ref[...] = total[half:].astype(bf16)


def finish_kernel(held_a_ref, part_a_ref, held_b_ref, part_b_ref, raw_ref, out_ref):
    half = held_a_ref.shape[0]
    for kind, held, part in ((0, held_a_ref, part_a_ref), (1, held_b_ref, part_b_ref)):
        here = pl.ds(kind * half, half)
        grad = held[...] + part[...].astype(f32)
        unit, length = normalize_rows(raw_ref[here])
        along = jnp.sum(unit * grad, axis=-1, keepdims=True)
        out_ref[here] = (grad - unit * along) / length


def shape(*dims, dtype=f32):
    return jax.ShapeDtypeStruct(dims, dtype)


def call(kernel, out_shape, *operands, mib=12, fetched=(), held=(), scratch=()):
    operands = [
        pltpu.with_memory_space_constraint(x, pltpu.HBM) if i in held else x
        for i, x in enumerate(operands)
    ]
    kept = pl.BlockSpec(memory_space=pltpu.VMEM)
    there = pl.BlockSpec(memory_space=pl.ANY)
    return pl.pallas_call(
        kernel,
        out_shape=out_shape,
        in_specs=[there if i in (*fetched, *held) else kept for i in range(len(operands))],
        out_specs=jax.tree.map(lambda _: kept, out_shape, is_leaf=lambda x: hasattr(x, 'shape')),
        scratch_shapes=[
            *(pltpu.VMEM(operands[i].shape, operands[i].dtype) for i in fetched),
            *(pltpu.SemaphoreType.DMA(()) for _ in fetched),
            *scratch,
        ],
        compiler_params=pltpu.CompilerParams(vmem_limit_bytes=mib << 20),
    )(*operands)


def fetch(sources, buffers, semaphores):
    copies = [pltpu.make_async_copy(*each) for each in zip(sources, buffers, semaphores)]
    for copy in copies:
        copy.start()
    return copies


def on_device(embeddings, codes, prototypes):
    n_proto = lax.axis_size(block)
    own_images, _, crops, features = embeddings.shape
    images = own_images * n_proto
    rows = images * crops
    own_rows = own_images * crops
    code = codes[:, 0]
    half = prototypes.shape[1] // 2

    *halves, by_crop, spread_emb = call(
        split_kernel,
        [
            shape(half, features, dtype=bf16),
            shape(half, features, dtype=bf16),
            shape(crops, own_images, features, dtype=bf16),
            shape(n_proto // 2, own_rows, features, dtype=bf16),
        ],
        prototypes[0], embeddings[:, 0],
        fetched=(0, 1), held=(0, 1),
    )
    for distance in (1, 3):
        moved = []
        for kind in kinds:
            moved.append(exchange(halves[kind], kind, distance))
        halves = [jnp.concatenate(pair) for pair in zip(halves, moved)]
    own_core = lax.all_to_all(spread_emb, "z", 0, 0)
    other_core = lax.ppermute(own_core, "core", [(0, 1), (1, 0)])
    gathered = {0: halves}
    for d in arrivals:
        gathered[d] = []
        for kind in kinds:
            gathered[d].append(exchange(halves[kind], 1 - kind, d))

    code = call(
        stage_kernel,
        pltpu.VMEM(code.shape, code.dtype),
        code,
        held=(0,),
        scratch=[pltpu.SemaphoreType.DMA((8,))],
    )
    z_t, local_sum, outgoing = call(
        embeddings_kernel,
        (shape(features, rows, dtype=bf16), shape(images, features), shape(images, features)),
        *(
            each.reshape(n_proto // 2, crops, own_images, features)
            for each in (own_core, other_core)
        ),
    )

    exponents = {}
    soft, own_sums, sums = [], [], []
    for d in (0, *arrivals):
        before = (*own_sums, *sums, outgoing) if d == arrivals[-1] else ()
        total_dims = (n_proto, rows // 128, 128) if before else (8, rows)
        own_dims = (2, images, features) if before else (images, features)
        *exponents[d], soft_part, own_term, totals = call(
            functools.partial(scores_kernel, distance=d, n_before=len(before) // 2),
            [shape(side * half, rows, dtype=bf16)] * 2
            + [shape(features, rows), shape(*own_dims), shape(*total_dims)],
            z_t, code, *gathered[d], *before,
        )
        soft.append(soft_part)
        own_sums.append(own_term)
        sums.append(totals)
    other_term = swapped(own_term)
    totals = lax.all_to_all(totals, block, 0, 0)

    arrived = [[], []]
    for d in (*arrivals, 0):
        first = d == arrivals[0]
        outs = call(
            functools.partial(
                prototypes_kernel,
                distance=d, crops=crops, own_images=own_images, first=first,
            ),
            [shape(side * half, features, dtype=bf16 if d else f32)] * 2
            + [shape(features, rows, dtype=bf16), shape(images, features, dtype=bf16)] * first,
            code, *((totals, z_t, local_sum, other_term) if first else (zw, target)),
            *exponents[d],
        )
        parts = outs[:2]
        if first:
            zw, target = outs[2:]
        for kind in kinds:
            if d:
                arrived[kind].append(exchange(parts[kind], 1 - kind, d))
            else:
                arrived[kind].insert(0, parts[kind])

    row_shape = (n_proto // 2, crops, own_images, features)
    kept_rows, sent_rows = call(
        functools.partial(rows_kernel, crops=crops, own_images=own_images),
        [shape(*row_shape), shape(*row_shape, dtype=bf16)],
        totals, own_term, other_term, *soft,
    )
    sent_rows = lax.ppermute(sent_rows, "core", [(0, 1), (1, 0)])
    held_parts = [arrived[kind][0] for kind in kinds]
    kept_rows, *held_parts = lax.optimization_barrier((kept_rows, *held_parts))
    for kind in kinds:
        arrived[kind][0] = held_parts[kind]
    row_parts = call(add_kernel, shape(*row_shape, dtype=bf16), kept_rows, sent_rows)
    row_parts = lax.all_to_all(row_parts, "z", 0, 0)

    held = []
    for kind in kinds:
        keep, send = call(
            far_sum_kernel,
            [shape(2 * half, features), shape(2 * half, features, dtype=bf16)],
            *arrived[kind],
        )
        held.append((keep, exchange(send, kind, 3)))
    operands = []
    for kind, (keep, part) in zip(kinds, held):
        keep, send = call(
            near_sum_kernel,
            [shape(half, features), shape(half, features, dtype=bf16)],
            keep, part,
        )
        operands += [keep, exchange(send, kind, 1)]
    grad_proto = call(finish_kernel, shape(*prototypes.shape[1:]), *operands, prototypes[0])

    grad_emb = call(
        finish_rows_kernel, shape(own_images, crops, features), row_parts, by_crop
    )
    return (grad_emb[:, None], grad_proto[None])


def solution(mesh):
    n_dp, n_proto, n_crop = mesh.devices.shape
    fine = Mesh(mesh.devices.reshape(n_dp, n_proto // 2, 2, n_crop), ("dp", *block, "crop"))
    return jax.shard_map(
        on_device,
        mesh=fine,
        in_specs=(
            P(("dp", *block), "crop", None, None),
            P("dp", "crop", block),
            P(block, ("dp", "crop"), None),
        ),
        out_specs=(P(("dp", *block), "crop", None, None), P(block, ("dp", "crop"), None)),
        check_vma=False,
    )
```
